32 devices in a mesh: dom: 8 (over y, x, core), blk: 4 (over z).
Axes of the slice: x: 2, y: 2, z: 4, core: 2. Of those that a mesh axis runs over, the one named last changes fastest.
Arguments:
- features: bfloat16 [16384, 1024], P(('dom', 'blk')), may hold values from -6 to 6
- tiles: bfloat16 [64, 4, 256, 256], P(('dom', 'blk')), may hold values from -0.1875 to 0.1875
- tile_cols: int32 [64, 4], P(('dom', 'blk')), may hold values from 0 to 1
- send_rows: int32 [32, 8, 128], P(('dom', 'blk')), may hold values from 0 to 511
- recv_dst: int32 [32, 8, 128], P(('dom', 'blk')), may hold values from 0 to 511
- recv_weight: float32 [32, 8, 128], P(('dom', 'blk')), may hold values from 0.1 to 1
- recv_count: int32 [32, 8], P(('dom', 'blk')), may hold values from 0 to 128, as said below
- weight: bfloat16 [1024, 1024], replicated, may hold values from -0.1875 to 0.1875
- bias: float32 [1024], replicated, may hold values from -3 to 3
Outputs:
- activated: bfloat16 [16384, 1024], P(('dom', 'blk'))
The draws below stay inside these ranges and needn't reach their ends.
Inputs may be any that keep to these rules, and one draw needn't show every extreme that they name: recv_count is zero for a panel's own partition; exactly one panel has 128 from every other partition, and every other panel's counts are at most 64.
All inputs are finite; a program needn't handle non-finite values.
Results may differ from the reference program's by a relative error of at most 0.0047.
Values may be sent and summed in bfloat16 or wider, within the bound.
A program may use at most 64 MiB of HBM per device.

```python
import math
import jax
import jax.numpy as jnp
from jax import lax

F = 1024
BLOCK = 256
PAIR_ROWS = 128
RB = 2
ROWS_DEV = 512
PARTS_SIZE = 8
GROUP = 4
PANELS = 32
NODES = 16384


def draw_recv_count(key, part):
    key_level, key_spread, key_heavy = jax.random.split(jax.random.fold_in(key, 11), 3)
    level = jax.random.randint(key_level, (PANELS, 1), 1, 5)
    lower = level * PAIR_ROWS // 16
    upper = level * PAIR_ROWS // 8
    spread = jax.random.randint(key_spread, (PANELS, PARTS_SIZE), 0, PAIR_ROWS + 1)
    counted = lower + spread % (upper - lower + 1)
    heavy = jax.random.randint(key_heavy, (), 0, PANELS)
    panel_ids = jnp.arange(PANELS)[:, None]
    counted = jnp.where(panel_ids == heavy, PAIR_ROWS, counted)
    own_part = panel_ids // GROUP == jnp.arange(PARTS_SIZE)[None, :]
    return jnp.where(own_part, 0, counted).astype(jnp.int32)


def with_ends(values, stream_key, smallest, top_value):
    longest = values.shape.index(max(values.shape))
    spots = []
    for shift in (0, 1):
        where = [jax.random.randint(jax.random.fold_in(stream_key, axis), (), 0, length) for axis, length in enumerate(values.shape)]
        where[longest] = (where[longest] + shift) % values.shape[longest]
        spots.append(tuple(where))
    return values.at[spots[0]].set(smallest).at[spots[1]].set(top_value)


def block_levels(own_key, extent, pieces, least, high):
    def one(position, blocks):
        steps = jax.random.uniform(jax.random.fold_in(jax.random.fold_in(own_key, 6), position), (blocks,), jnp.float32, least / len(pieces), high / len(pieces))
        return jnp.repeat(jnp.exp(steps), extent[position] // blocks).reshape((-1,) + (1,) * (len(extent) - position - 1))

    gain = one(*pieces[0])
    for cut in pieces[1:]:
        gain = gain * one(*cut)
    return gain


def scatter_about(rng, extent, scale, bound, cuts=(), kind=jnp.bfloat16):
    entries = scale * jax.random.normal(rng, extent, jnp.float32)
    if cuts:
        entries = entries * block_levels(rng, extent, cuts, -0.22, 0.18)
    return jnp.clip(entries, -bound, bound).astype(kind)


def setup_inputs(seed: int = 0) -> dict:
    key_of = jax.random.split(jax.random.key(seed), 10)
    features = scatter_about(key_of[0], (NODES, F), 1.0, 6.0, ((0, 32),))
    tiles = scatter_about(key_of[1], (PANELS * RB, GROUP, BLOCK, BLOCK), (GROUP * BLOCK) ** -0.5, 0.1875, ((0, 32),))
    tile_cols = with_ends(jax.random.randint(key_of[2], (PANELS * RB, GROUP), 0, RB), jax.random.fold_in(key_of[2], 1), 0, RB - 1).astype(jnp.int32)
    send_rows = with_ends(jax.random.randint(key_of[3], (PANELS, PARTS_SIZE, PAIR_ROWS), 0, ROWS_DEV), jax.random.fold_in(key_of[3], 1), 0, ROWS_DEV - 1).astype(jnp.int32)
    recv_dst = with_ends(jax.random.randint(key_of[4], (PANELS, PARTS_SIZE, PAIR_ROWS), 0, ROWS_DEV), jax.random.fold_in(key_of[4], 1), 0, ROWS_DEV - 1).astype(jnp.int32)
    recv_weight = jnp.clip(jnp.exp(math.log(1.0) - 2.3025851 * jax.random.uniform(key_of[5], (PANELS, PARTS_SIZE, PAIR_ROWS), jnp.float32) ** block_levels(key_of[5], (PANELS, PARTS_SIZE, PAIR_ROWS), ((0, 32),), -0.2, 0.2)), 0.1, 1.0)
    recv_count = draw_recv_count(jax.random.fold_in(key_of[9], 71), 0)
    weight = scatter_about(key_of[7], (F, F), F ** -0.5, 0.1875)
    bias = scatter_about(key_of[8], (F,), 0.5, 3.0, (), jnp.float32)
    return dict(features=features, tiles=tiles, tile_cols=tile_cols, send_rows=send_rows, recv_dst=recv_dst, recv_weight=recv_weight, recv_count=recv_count, weight=weight, bias=bias)


def reference(features, tiles, tile_cols, send_rows, recv_dst, recv_weight, recv_count, weight, bias):
    feat_blocks = features.reshape(PARTS_SIZE, GROUP, RB, BLOCK, F)
    flat_panels = features.reshape(PARTS_SIZE, GROUP, ROWS_DEV, F)
    all_tiles = tiles.reshape(PARTS_SIZE, GROUP * RB, GROUP, BLOCK, BLOCK)
    all_cols = tile_cols.reshape(PARTS_SIZE, GROUP * RB, GROUP)
    all_sends = send_rows.reshape(PARTS_SIZE, GROUP, PARTS_SIZE, PAIR_ROWS)
    all_dst = recv_dst.reshape(PARTS_SIZE, GROUP, PARTS_SIZE * PAIR_ROWS)
    all_weights = recv_weight.reshape(PARTS_SIZE, GROUP, PARTS_SIZE, PAIR_ROWS)
    all_counts = recv_count.reshape(PARTS_SIZE, GROUP, PARTS_SIZE)
    slot_ids = jnp.arange(PAIR_ROWS)
    row_ids = jnp.arange(ROWS_DEV)

    def per_partition(partition):
        part_feat = feat_blocks[partition]
        sources = jnp.arange(GROUP)[None, :]
        picked = part_feat[sources, all_cols[partition]]
        inner = jnp.einsum('rsij,rsjf->rif', all_tiles[partition].astype(jnp.float32), picked.astype(jnp.float32))
        inner = inner.reshape(GROUP, ROWS_DEV, F)
        listed = all_sends[:, :, partition, :]
        source_part = jnp.arange(PARTS_SIZE)[:, None, None]
        place_idx = jnp.arange(GROUP)[None, :, None]
        rows_in = flat_panels[source_part, place_idx, listed]
        rows_in = jnp.transpose(rows_in, (1, 0, 2, 3)).reshape(GROUP, PARTS_SIZE * PAIR_ROWS, F)
        in_use = slot_ids[None, None, :] < all_counts[partition][:, :, None]
        edge_weight = jnp.where(in_use, all_weights[partition], jnp.float32(0.0)).astype(jnp.bfloat16)
        edge_weight = edge_weight.reshape(GROUP, 1, PARTS_SIZE * PAIR_ROWS)
        hits = all_dst[partition][:, None, :] == row_ids[None, :, None]
        placed = jnp.where(hits, edge_weight.astype(jnp.float32), jnp.float32(0.0))
        boundary = jnp.einsum('grk,gkf->grf', placed, rows_in.astype(jnp.float32))
        aggregated = (inner + boundary).astype(jnp.bfloat16)
        result = jnp.dot(aggregated.reshape(GROUP * ROWS_DEV, F), weight, preferred_element_type=jnp.float32)
        return jax.nn.relu(result + bias.astype(jnp.float32)).astype(jnp.bfloat16)

    return lax.map(per_partition, jnp.arange(PARTS_SIZE)).reshape(NODES, F)
```

```python
import functools

import jax
import jax.numpy as jnp
from jax import lax
from jax.experimental import pallas as pl
from jax.experimental.pallas import tpu as pltpu
from jax.sharding import PartitionSpec as P

CHUNK = 128
OUT_TILE = 256
F32 = jnp.float32
BF16 = jnp.bfloat16


def dot(a, b):
    return jnp.dot(a, b, preferred_element_type=F32)


def line_kernel(
    parts,
    feat,
    tiles,
    cols_hbm,
    send_hbm,
    dst_hbm,
    edge_hbm,
    count_hbm,
    weight,
    bias_hbm,
    out,
    cols,
    send_rows,
    recv_dst,
    recv_weight,
    recv_count,
    bias,
    x_own,
    x_par,
    x_om,
    x_oe,
    t_own,
    t_par,
    c_own,
    c_par,
    a_own,
    a_par,
    acc,
    acc_p,
    p_out,
    p_in,
    outgoing,
    incoming,
    place,
    w_vmem,
    agg,
    total,
    load_sem,
    tile_send,
    tile_recv,
    x_send,
    x_recv,
    om_send,
    om_recv,
    relay_send,
    relay_recv,
    p_send,
    p_recv,
    row_send,
    row_recv,
    y_send,
    y_recv,
    end_in,
    mids_in,
    rows_in,
):
    me = lax.axis_index("dom")
    b = lax.axis_index("blk")
    is_end = (b == 0) | (b == 3)
    is_mid = jnp.logical_not(is_end)
    core = lax.rem(me, 2)
    partner = b + 1 - 2 * lax.rem(b, 2)
    across = 3 - b
    far = 3 - partner
    rows, width = x_own.shape
    side = t_own.shape[2]
    blocks = t_own.shape[0]
    slots = outgoing.shape[1]
    chunks = width // CHUNK
    half = rows // 2

    def col(c):
        return pl.ds(pl.multiple_of(c * CHUNK, CHUNK), CHUNK)

    def remote(src, dst, send, recv, target):
        return pltpu.make_async_remote_copy(
            src_ref=src,
            dst_ref=dst,
            send_sem=send,
            recv_sem=recv,
            device_id=target,
            device_id_type=pl.DeviceIdType.MESH,
        )

    def x_copy(c):
        return remote(feat.at[:, col(c)], x_par.at[:, col(c)], x_send.at[c], x_recv.at[c], {"blk": partner})

    def y_copy(c):
        return remote(feat.at[:, col(c)], x_par.at[:, col(c)], y_send.at[c], y_recv.at[c], {"blk": partner})

    def om_copy(c):
        return remote(feat.at[:, col(c)], x_om.at[:, col(c)], om_send.at[c], om_recv.at[c], {"blk": across})

    def relay_copy(c):
        return remote(x_par.at[:, col(c)], x_oe.at[:, col(c)], relay_send.at[c], relay_recv.at[c], {"blk": across})

    def p_copy(c, h):
        at = pl.ds(h * half, half)
        return remote(p_out.at[at, col(c)], p_in.at[at, col(c)], p_send.at[2 * c + h], p_recv.at[2 * c + h], {"blk": partner})

    def tile_copy(j):
        source = (far, across)[j]
        return remote(t_own.at[:, source], t_par.at[j], tile_send.at[j], tile_recv.at[j], {"blk": partner})

    def cols_copy():
        return remote(c_own, c_par, tile_send.at[2], tile_recv.at[2], {"blk": partner})

    def row_copy(q, source):
        return remote(outgoing.at[q], incoming.at[pl.ds(pl.multiple_of(source * slots, slots), slots)], row_send.at[q], row_recv.at[source], {"dom": q})

    def load(j, src, dst):
        return pltpu.make_async_copy(src, dst, load_sem.at[j])

    load_cols = load(0, cols_hbm, cols)
    load_x = load(1, feat, x_own)
    load_t = load(2, tiles, t_own)
    load_small = [
        load(3, send_hbm, send_rows),
        load(4, dst_hbm, recv_dst),
        load(5, edge_hbm, recv_weight),
        load(6, count_hbm, recv_count),
        load(7, bias_hbm, bias),
    ]
    load_w = load(8, weight, w_vmem)
    for copy in [load_cols, load_x, load_t] + load_small:
        copy.start()

    def signal(semaphore, target):
        pl.semaphore_signal(semaphore, inc=1, device_id=target, device_id_type=pl.DeviceIdType.MESH)

    def others(act):
        @pl.loop(1, parts)
        def _(k):
            act({"dom": lax.rem(me + k, parts)})

    barrier = pltpu.get_barrier_semaphore()

    @pl.when(is_mid)
    def _():
        signal(barrier, {"blk": across})
        signal(barrier, {"blk": partner})
        pl.semaphore_wait(barrier, 1)

        @pl.when(core == 1)
        def _():
            load_x.wait()

        @pl.loop(0, chunks)
        def _(c):
            om_copy(c).start()

        pl.semaphore_wait(end_in, 1)

        @pl.loop(0, chunks)
        def _(c):
            y_copy(c).start()

    load_cols.wait()
    for r in range(blocks):
        for s in range(4):
            c_own[pl.ds(r * 4 + s, 1), :] = jnp.full((1, side), cols[r, s], jnp.int32)

    @pl.when(is_end)
    def _():
        others(lambda target: signal(barrier, target))
        load_t.wait()
        pl.semaphore_wait(barrier, parts)
        signal(end_in, {"blk": partner})
        cols_copy().start()
        for j in range(2):
            tile_copy(j).start()

        @pl.loop(0, chunks)
        def _(c):
            x_copy(c).start()

        others(lambda target: signal(mids_in, target))

    @pl.when(is_end | (core == 0))
    def _():
        load_x.wait()

    load_w.start()
    for copy in load_small:
        copy.wait()


    @pl.when(is_end)
    def _():
        pl.semaphore_wait(mids_in, parts - 1)
        signal(rows_in, {"blk": partner})

    @pl.when(is_mid)
    def _():
        pl.semaphore_wait(rows_in, 1)

    row_ids = lax.broadcasted_iota(jnp.int32, (rows, slots), 0)
    slot_ids = lax.broadcasted_iota(jnp.int32, (1, slots), 1)

    @pl.loop(1, parts + 1)
    def _(k):
        q = lax.rem(me + k, parts)
        listed = send_rows[0, pl.ds(q, 1), :]
        hot = jnp.where(row_ids == listed, F32(1.0), F32(0.0)).astype(BF16)
        picked = lax.dot_general(hot, x_own[...], (((0,), (0,)), ((), ())), preferred_element_type=F32)

        @pl.when(k < parts)
        def _():
            outgoing[q] = picked.astype(BF16)
            row_copy(q, me).start()

        @pl.when(k == parts)
        def _():
            incoming[pl.ds(pl.multiple_of(me * slots, slots), slots), :] = picked.astype(BF16)

    for q in range(parts):
        used = jnp.where(slot_ids < recv_count[0, q], recv_weight[0, q : q + 1, :], F32(0.0))
        hit = row_ids == recv_dst[0, q : q + 1, :]
        place[:, q * slots : (q + 1) * slots] = jnp.where(hit, used, F32(0.0)).astype(BF16)

    @pl.when(is_mid)
    def _():
        load_t.wait()

    def spread(target, at, matrix, picked, r):
        zero = jnp.zeros_like(matrix)
        mask = jnp.broadcast_to(picked, matrix.shape)
        for block in range(blocks):
            start = at * rows + block * side
            target[r * side : (r + 1) * side, start : start + side] = jnp.where(mask == block, matrix, zero)

    def own_tiles(at, source):
        for r in range(blocks):
            spread(a_own, at, t_own[r, source], c_own[pl.ds(r * 4 + source, 1), :], r)

    def wait_rows():
        @pl.loop(1, parts)
        def _(k):
            source = lax.rem(me + k, parts)
            row_copy(source, source).wait_recv()

    own_tiles(1, b)
    load_w.wait()
    pair = 2 * CHUNK
    pairs = width // pair

    def add_product(p):
        at = pl.ds(pl.multiple_of(p * pair, pair), pair)
        term = dot(agg[:, at], w_vmem[at, :])

        @pl.when(p == 0)
        def _():
            total[...] = term

        @pl.when(p > 0)
        def _():
            total[...] += term

    @pl.when(is_mid)
    def _():
        own_tiles(0, partner)
        own_tiles(2, across)
        own_tiles(3, far)
        cols_copy().wait_recv()
        for j in range(2):
            tile_copy(j).wait_recv()
            source = (across, far)[j]
            for r in range(blocks):
                spread(a_par, j, t_par[j, r], c_par[pl.ds(r * 4 + source, 1), :], r)

        @pl.loop(0, chunks + 2)
        def _(step):
            @pl.when(step < chunks)
            def _():
                at = col(step)
                x_copy(step).wait_recv()
                relay_copy(step).start()
                om_copy(step).wait_recv()
                own = x_own[:, at]
                other = x_om[:, at]
                acc_p[:, at] = dot(a_par[:, :rows], other)
                acc[:, at] = (
                    dot(a_own[:, :rows], x_par[:, at])
                    + dot(a_own[:, rows : 2 * rows], own)
                    + dot(a_own[:, 2 * rows : 3 * rows], other)
                )

            @pl.when(step == 2)
            def _():
                wait_rows()

            @pl.when(step >= 2)
            def _():
                c = step - 2
                at = col(c)
                mine = acc[:, at] + dot(place[...], incoming[:, at])
                acc[:, at] = mine
                relay_copy(c).wait_recv()
                last = x_oe[:, at]
                for h in range(2):
                    part = slice(h * half, (h + 1) * half)
                    p_out[part, at] = (acc_p[part, at] + dot(a_par[part, rows:], last)).astype(BF16)
                    p_copy(c, h).start()
                agg[:, at] = (acc[:, at] + dot(a_own[:, 3 * rows :], last)).astype(BF16)

                @pl.when((lax.rem(c, 2) == 1) & (c < chunks - 1))
                def _():
                    add_product(c // 2)

    @pl.when(is_end)
    def _():
        own_tiles(0, partner)
        wait_rows()

        @pl.loop(0, chunks)
        def _(c):
            at = col(c)
            y_copy(c).wait_recv()
            acc[:, at] = (
                dot(a_own[:, rows : 2 * rows], x_own[:, at])
                + dot(a_own[:, :rows], x_par[:, at])
                + dot(place[...], incoming[:, at])
            )

        @pl.loop(0, chunks - 1)
        def _(c):
            at = col(c)
            for h in range(2):
                p_copy(c, h).wait_recv()
            agg[:, at] = (acc[:, at] + p_in[:, at].astype(F32)).astype(BF16)

            @pl.when(lax.rem(c, 2) == 1)
            def _():
                add_product(c // 2)

    for h in range(2):
        part = slice(h * half, (h + 1) * half)

        @pl.when(is_end)
        def _():
            at = slice((chunks - 1) * CHUNK, chunks * CHUNK)
            p_copy(chunks - 1, h).wait_recv()
            agg[part, at] = (acc[part, at] + p_in[part, at].astype(F32)).astype(BF16)

        @pl.loop(0, width // OUT_TILE)
        def _(t):
            at = pl.ds(pl.multiple_of(t * OUT_TILE, OUT_TILE), OUT_TILE)
            last = slice((pairs - 1) * pair, pairs * pair)
            result = total[part, at] + dot(agg[part, last], w_vmem[last, at]) + bias[:, at]
            out[part, at] = jnp.maximum(result, F32(0.0)).astype(BF16)

    @pl.loop(1, parts)
    def _(k):
        row_copy(lax.rem(me + k, parts), me).wait_send()

    @pl.when(is_mid)
    def _():
        @pl.loop(0, chunks)
        def _(c):
            om_copy(c).wait_send()
            y_copy(c).wait_send()
            relay_copy(c).wait_send()
            p_copy(c, 0).wait_send()
            p_copy(c, 1).wait_send()

    @pl.when(is_end)
    def _():
        cols_copy().wait_send()
        for j in range(2):
            tile_copy(j).wait_send()

        @pl.loop(0, chunks)
        def _(c):
            x_copy(c).wait_send()


def line_layer(features, tiles, tile_cols, send_rows, recv_dst, recv_weight, recv_count, weight, bias):
    parts = lax.axis_size("dom")
    rows, width = features.shape
    blocks, group, side, _ = tiles.shape
    slots = send_rows.shape[2]
    chunks = width // CHUNK
    out_width = weight.shape[1]
    hbm = pl.BlockSpec(memory_space=pltpu.HBM)
    dma = pltpu.SemaphoreType.DMA
    panel = pltpu.VMEM((rows, width), BF16)
    return pl.pallas_call(
        functools.partial(line_kernel, parts),
        out_shape=jax.ShapeDtypeStruct((rows, out_width), BF16),
        in_specs=[hbm] * 9,
        out_specs=pl.BlockSpec(memory_space=pltpu.VMEM),
        scratch_shapes=[
            pltpu.SMEM(tile_cols.shape, jnp.int32),
            pltpu.VMEM(send_rows.shape, jnp.int32),
            pltpu.VMEM(recv_dst.shape, jnp.int32),
            pltpu.VMEM(recv_weight.shape, F32),
            pltpu.SMEM(recv_count.shape, jnp.int32),
            pltpu.VMEM((1, out_width), F32),
            panel,
            panel,
            panel,
            panel,
            pltpu.VMEM(tiles.shape, BF16),
            pltpu.VMEM((2, blocks, side, side), BF16),
            pltpu.VMEM((blocks * group, side), jnp.int32),
            pltpu.VMEM((blocks * group, side), jnp.int32),
            pltpu.VMEM((rows, 4 * rows), BF16),
            pltpu.VMEM((rows, 2 * rows), BF16),
            pltpu.VMEM((rows, width), F32),
            pltpu.VMEM((rows, width), F32),
            panel,
            panel,
            pltpu.VMEM((parts, slots, width), BF16),
            pltpu.VMEM((parts * slots, width), BF16),
            pltpu.VMEM((rows, parts * slots), BF16),
            pltpu.VMEM(weight.shape, BF16),
            panel,
            pltpu.VMEM((rows, out_width), F32),
            dma((9,)),
            dma((3,)),
            dma((3,)),
        ]
        + [dma((chunks,))] * 6
        + [dma((2 * chunks,))] * 2
        + [dma((parts,))] * 2
        + [dma((chunks,))] * 2
        + [pltpu.SemaphoreType.REGULAR] * 3,
        compiler_params=pltpu.CompilerParams(collective_id=0, has_side_effects=True, vmem_limit_bytes=48 << 20),
    )(*(pltpu.with_memory_space_constraint(a, pltpu.HBM) for a in (features, tiles, tile_cols, send_rows, recv_dst, recv_weight, recv_count, weight, bias.reshape(1, -1))))


def shifted(array, axis, by):
    size = lax.axis_size(axis)
    return lax.ppermute(array, axis, [(i, (i + by) % size) for i in range(size)])


def ring_layer(features, tiles, tile_cols, send_rows, recv_dst, recv_weight, recv_count, weight, bias):
    cycle_size = lax.axis_size("blk")
    position = lax.axis_index("blk")
    row_blocks = tiles.shape[0]
    tile_rows = tiles.shape[2]
    feature_width = features.shape[1]
    panel_rows = features.shape[0]

    def product(current, source):
        picked = lax.dynamic_index_in_dim(tile_cols, source, 1, keepdims=False)
        matrices = lax.dynamic_index_in_dim(tiles, source, 1, keepdims=False)
        pieces = []
        for row_block in range(row_blocks):
            start = picked[row_block] * tile_rows
            chosen = lax.dynamic_slice_in_dim(current, start, tile_rows, 0)
            pieces.append(jnp.dot(matrices[row_block], chosen, preferred_element_type=jnp.float32))
        return jnp.concatenate(pieces, axis=0)

    summed = product(features, position)

    def advance(rotation, state_carry):
        current, running = state_carry
        current = shifted(current, "blk", 1)
        return (current, running + product(current, (position - rotation) % cycle_size))

    _, summed = lax.fori_loop(1, cycle_size, advance, (features, summed))
    outgoing = features[send_rows[0]]
    incoming = lax.all_to_all(outgoing, "dom", split_axis=0, concat_axis=0, tiled=True)
    slot_ids = jnp.arange(incoming.shape[1])
    in_use = slot_ids[None, :] < recv_count[0][:, None]
    edge_weight = (
        jnp.where(in_use, recv_weight[0], jnp.float32(0.0)).astype(jnp.bfloat16).reshape(1, -1)
    )
    targets = recv_dst[0].reshape(1, -1)
    local_rows = jnp.arange(panel_rows)[:, None]
    placement_matrix = jnp.where(targets == local_rows, edge_weight, jnp.zeros_like(edge_weight))
    summed = summed + jnp.dot(
        placement_matrix, incoming.reshape(-1, feature_width), preferred_element_type=jnp.float32
    )
    aggregated = summed.astype(jnp.bfloat16)
    result = jnp.dot(aggregated, weight, preferred_element_type=jnp.float32) + bias
    return jax.nn.relu(result).astype(jnp.bfloat16)


def solution(mesh):
    in_specs = (
        P(("dom", "blk"), None),
        P(("dom", "blk"), None, None, None),
        P(("dom", "blk"), None),
        P(("dom", "blk"), None, None),
        P(("dom", "blk"), None, None),
        P(("dom", "blk"), None, None),
        P(("dom", "blk"), None),
        P(),
        P(),
    )
    out_specs = P(("dom", "blk"), None)
    layer = line_layer if mesh.shape["blk"] == 4 else ring_layer
    return jax.shard_map(layer, mesh=mesh, in_specs=in_specs, out_specs=out_specs, check_vma=False)
```

```python
import functools

import jax
import jax.numpy as jnp
from jax import lax
from jax.experimental import pallas as pl
from jax.experimental.pallas import tpu as pltpu
from jax.sharding import PartitionSpec as P

CHUNK = 128
OUT_TILE = 256
F32 = jnp.float32
BF16 = jnp.bfloat16


def dot(a, b):
    return jnp.dot(a, b, preferred_element_type=F32)


def line_kernel(
    parts,
    feat,
    tiles,
    cols_hbm,
    send_hbm,
    dst_hbm,
    edge_hbm,
    count_hbm,
    weight,
    bias_hbm,
    out,
    cols,
    send_rows,
    recv_dst,
    recv_weight,
    recv_count,
    bias,
    x_own,
    x_par,
    x_om,
    x_oe,
    t_own,
    t_par,
    c_own,
    c_par,
    a_own,
    a_par,
    acc,
    acc_p,
    acc_r,
    p_out,
    p_in,
    outgoing,
    incoming,
    place,
    w_vmem,
    agg,
    total,
    load_sem,
    sent,
    first,
    second,
    third,
    tile_recv,
    row_send,
    row_recv,
    end_in,
    mids_in,
    rows_in,
):
    me = lax.axis_index("dom")
    b = lax.axis_index("blk")
    is_end = (b == 0) | (b == 3)
    is_mid = jnp.logical_not(is_end)
    partner = b + 1 - 2 * lax.rem(b, 2)
    across = 3 - b
    far = 3 - partner
    rows, width = x_own.shape
    side = t_own.shape[2]
    blocks = t_own.shape[0]
    slots = outgoing.shape[1]
    chunks = width // CHUNK
    half = rows // 2

    def col(c):
        return pl.ds(pl.multiple_of(c * CHUNK, CHUNK), CHUNK)

    def remote(src, dst, send, recv, target):
        return pltpu.make_async_remote_copy(
            src_ref=src,
            dst_ref=dst,
            send_sem=send,
            recv_sem=recv,
            device_id=target,
            device_id_type=pl.DeviceIdType.MESH,
        )

    def panel_copy(src, dst, send, recv, at, target):
        return remote(src.at[at], dst.at[at], sent.at[send], recv, {"blk": target})

    def chunk(c):
        return (slice(None), col(c))

    def x_copy(c):
        return panel_copy(feat, x_par, 0, first.at[c], chunk(c), partner)

    def tile_copy(j):
        source = (far, across)[j]
        return remote(tiles.at[:, source], t_par.at[j], sent.at[1 + j], tile_recv.at[j], {"blk": partner})

    def cols_copy():
        return remote(c_own, c_par, sent.at[3], tile_recv.at[2], {"blk": partner})

    def om_copy(c):
        return panel_copy(feat, x_om, 0, second.at[c], chunk(c), across)

    def relay_copy(c):
        return panel_copy(x_par, x_oe, 1, third.at[c], chunk(c), across)

    def y_copy(c):
        return panel_copy(feat, x_par, 2, third.at[c], chunk(c), partner)

    def p_copy(c, h):
        recv = (first, second)[h].at[c]
        return panel_copy(p_out, p_in, 3, recv, (pl.ds(h * half, half), col(c)), partner)

    def all_sent(j, buffer):
        return pltpu.make_async_copy(buffer, buffer, sent.at[j])

    def row_copy(q, k, source):
        return remote(outgoing.at[q], incoming.at[pl.ds(pl.multiple_of(source * slots, slots), slots)], row_send.at[k], row_recv, {"dom": q})

    def load(j, src, dst):
        return pltpu.make_async_copy(src, dst, load_sem.at[j])

    load_cols = load(0, cols_hbm, cols)
    load_x = load(1, feat, x_own)
    load_t = load(2, tiles, t_own)
    load_small = [
        load(3, send_hbm, send_rows),
        load(4, dst_hbm, recv_dst),
        load(5, edge_hbm, recv_weight),
        load(6, count_hbm, recv_count),
        load(7, bias_hbm, bias),
    ]
    load_w = load(8, weight, w_vmem)

    def signal(semaphore, target):
        pl.semaphore_signal(semaphore, inc=1, device_id=target, device_id_type=pl.DeviceIdType.MESH)

    def others(act):
        @pl.loop(1, parts)
        def _(k):
            act({"dom": lax.rem(me + k, parts)})

    barrier = pltpu.get_barrier_semaphore()

    @pl.when(is_mid)
    def _():
        signal(barrier, {"blk": across})
        signal(barrier, {"blk": partner})
        pl.semaphore_wait(barrier, 1)

        @pl.loop(0, chunks)
        def _(c):
            om_copy(c).start()

    @pl.when(is_end)
    def _():
        others(lambda target: signal(barrier, target))

    for copy in [load_cols, load_x] + load_small + [load_t, load_w]:
        copy.start()

    @pl.when(is_mid)
    def _():
        pl.semaphore_wait(end_in, 1)

        @pl.loop(0, chunks)
        def _(c):
            y_copy(c).start()

    load_cols.wait()
    for r in range(blocks):
        for s in range(4):
            c_own[pl.ds(r * 4 + s, 1), :] = jnp.full((1, side), cols[r, s], jnp.int32)

    @pl.when(is_end)
    def _():
        pl.semaphore_wait(barrier, parts)
        signal(end_in, {"blk": partner})
        cols_copy().start()
        for j in range(2):
            tile_copy(j).start()

        @pl.loop(0, chunks)
        def _(c):
            x_copy(c).start()

        others(lambda target: signal(mids_in, target))

    for copy in [load_x] + load_small:
        copy.wait()


    @pl.when(is_end)
    def _():
        pl.semaphore_wait(mids_in, parts - 1)
        signal(rows_in, {"blk": partner})

    @pl.when(is_mid)
    def _():
        pl.semaphore_wait(rows_in, 1)

    row_ids = lax.broadcasted_iota(jnp.int32, (rows, slots), 0)
    slot_ids = lax.broadcasted_iota(jnp.int32, (1, slots), 1)

    @pl.loop(1, parts + 1)
    def _(k):
        q = lax.rem(me + k, parts)
        listed = send_rows[0, pl.ds(q, 1), :]
        hot = jnp.where(row_ids == listed, F32(1.0), F32(0.0)).astype(BF16)
        picked = lax.dot_general(hot, x_own[...], (((0,), (0,)), ((), ())), preferred_element_type=F32)

        @pl.when(k < parts)
        def _():
            outgoing[q] = picked.astype(BF16)


            row_copy(q, k, me).start()

        @pl.when(k == parts)
        def _():
            incoming[pl.ds(pl.multiple_of(me * slots, slots), slots), :] = picked.astype(BF16)

    for q in range(parts):
        used = jnp.where(slot_ids < recv_count[0, q], recv_weight[0, q : q + 1, :], F32(0.0))
        hit = row_ids == recv_dst[0, q : q + 1, :]
        place[:, q * slots : (q + 1) * slots] = jnp.where(hit, used, F32(0.0)).astype(BF16)

    load_t.wait()

    def spread(target, at, matrix, picked, r):
        zero = jnp.zeros_like(matrix)
        mask = jnp.broadcast_to(picked, matrix.shape)
        for block in range(blocks):
            start = at * rows + block * side
            target[r * side : (r + 1) * side, start : start + side] = jnp.where(mask == block, matrix, zero)

    def own_tiles(at, source):
        for r in range(blocks):
            spread(a_own, at, t_own[r, source], c_own[pl.ds(r * 4 + source, 1), :], r)

    def wait_rows():
        arrived = incoming.at[pl.ds(0, (parts - 1) * slots)]
        pltpu.make_async_copy(arrived, arrived, row_recv).wait()

    own_tiles(1, b)
    load_w.wait()
    pair = 2 * CHUNK
    pairs = width // pair

    def pair_at(p):
        return pl.ds(pl.multiple_of(p * pair, pair), pair)

    def add_product(p):
        at = pair_at(p)
        term = dot(agg[:, at], w_vmem[at, :])

        @pl.when(p == 0)
        def _():
            total[...] = term

        @pl.when(p > 0)
        def _():
            total[...] += term

    @pl.when(is_mid)
    def _():
        own_tiles(0, partner)
        own_tiles(2, across)
        own_tiles(3, far)
        cols_copy().wait_recv()
        for j in range(2):
            tile_copy(j).wait_recv()
            source = (across, far)[j]
            for r in range(blocks):
                spread(a_par, j, t_par[j, r], c_par[pl.ds(r * 4 + source, 1), :], r)

        @pl.loop(0, chunks + 2)
        def _(step):
            @pl.when(step < chunks)
            def _():
                at = col(step)
                x_copy(step).wait_recv()
                relay_copy(step).start()
                om_copy(step).wait_recv()
                own = x_own[:, at]
                other = x_om[:, at]
                acc_p[:, at] = dot(a_par[:, :rows], other)
                acc[:, at] = (
                    dot(a_own[:, :rows], x_par[:, at])
                    + dot(a_own[:, rows : 2 * rows], own)
                    + dot(a_own[:, 2 * rows : 3 * rows], other)
                )

            @pl.when(step >= 2)
            def _():
                c = step - 2
                at = col(c)
                relay_copy(c).wait_recv()
                last = x_oe[:, at]
                for h in range(2):
                    part = slice(h * half, (h + 1) * half)
                    p_out[part, at] = (acc_p[part, at] + dot(a_par[part, rows:], last)).astype(BF16)
                    p_copy(c, h).start()
                acc[:, at] += dot(a_own[:, 3 * rows :], last)

            @pl.when(step == 4)
            def _():
                wait_rows()

            @pl.when((step == 4) | (step == 5) | (step == 7))
            def _():
                p = jnp.minimum(step - 4, 2)
                at = pair_at(p)
                agg[:, at] = (acc[:, at] + dot(place[...], incoming[:, at])).astype(BF16)
                add_product(p)

            @pl.when(step == 6)
            def _():
                at = pair_at(pairs - 1)
                acc_r[...] = dot(place[...], incoming[:, at])

        at = pair_at(pairs - 1)
        agg[:, at] = (acc[:, at] + acc_r[...]).astype(BF16)

    @pl.when(is_end)
    def _():
        own_tiles(0, partner)

        @pl.loop(0, pairs)
        def _(p):
            at = pair_at(p)
            y_copy(2 * p).wait_recv()
            y_copy(2 * p + 1).wait_recv()
            acc[:, at] = dot(a_own[:, rows : 2 * rows], x_own[:, at]) + dot(a_own[:, :rows], x_par[:, at])

        wait_rows()

        @pl.loop(0, pairs)
        def _(p):
            at = pair_at(p)
            acc[:, at] += dot(place[...], incoming[:, at])

        @pl.loop(0, chunks - 1)
        def _(c):
            at = col(c)
            for h in range(2):
                p_copy(c, h).wait_recv()
            agg[:, at] = (acc[:, at] + p_in[:, at].astype(F32)).astype(BF16)

            @pl.when(lax.rem(c, 2) == 1)
            def _():
                add_product(c // 2)

    for h in range(2):
        part = slice(h * half, (h + 1) * half)

        @pl.when(is_end)
        def _():
            at = slice((chunks - 1) * CHUNK, chunks * CHUNK)
            p_copy(chunks - 1, h).wait_recv()
            agg[part, at] = (acc[part, at] + p_in[part, at].astype(F32)).astype(BF16)

        @pl.loop(0, width // OUT_TILE)
        def _(t):
            at = pl.ds(pl.multiple_of(t * OUT_TILE, OUT_TILE), OUT_TILE)
            last = slice((pairs - 1) * pair, pairs * pair)
            result = total[part, at] + dot(agg[part, last], w_vmem[last, at]) + bias[:, at]
            out[part, at] = jnp.maximum(result, F32(0.0)).astype(BF16)

    for k in range(1, parts):
        row_copy(lax.rem(me + k, parts), k, me).wait_send()

    all_sent(0, x_own).wait()

    @pl.when(is_mid)
    def _():
        for j in range(1, 4):
            all_sent(j, x_own).wait()

    @pl.when(is_end)
    def _():
        cols_copy().wait_send()
        for j in range(2):
            tile_copy(j).wait_send()


def line_layer(features, tiles, tile_cols, send_rows, recv_dst, recv_weight, recv_count, weight, bias):
    parts = lax.axis_size("dom")
    rows, width = features.shape
    blocks, group, side, _ = tiles.shape
    slots = send_rows.shape[2]
    chunks = width // CHUNK
    out_width = weight.shape[1]
    hbm = pl.BlockSpec(memory_space=pltpu.HBM)
    dma = pltpu.SemaphoreType.DMA
    panel = pltpu.VMEM((rows, width), BF16)
    return pl.pallas_call(
        functools.partial(line_kernel, parts),
        out_shape=jax.ShapeDtypeStruct((rows, out_width), BF16),
        in_specs=[hbm] * 9,
        out_specs=pl.BlockSpec(memory_space=pltpu.VMEM),
        scratch_shapes=[
            pltpu.SMEM(tile_cols.shape, jnp.int32),
            pltpu.VMEM(send_rows.shape, jnp.int32),
            pltpu.VMEM(recv_dst.shape, jnp.int32),
            pltpu.VMEM(recv_weight.shape, F32),
            pltpu.SMEM(recv_count.shape, jnp.int32),
            pltpu.VMEM((1, out_width), F32),
            panel,
            panel,
            panel,
            panel,
            pltpu.VMEM(tiles.shape, BF16),
            pltpu.VMEM((2, blocks, side, side), BF16),
            pltpu.VMEM((blocks * group, side), jnp.int32),
            pltpu.VMEM((blocks * group, side), jnp.int32),
            pltpu.VMEM((rows, 4 * rows), BF16),
            pltpu.VMEM((rows, 2 * rows), BF16),
            pltpu.VMEM((rows, width), F32),
            pltpu.VMEM((rows, width), F32),
            pltpu.VMEM((rows, 2 * CHUNK), F32),
            panel,
            panel,
            pltpu.VMEM((parts, slots, width), BF16),
            pltpu.VMEM((parts * slots, width), BF16),
            pltpu.VMEM((rows, parts * slots), BF16),
            pltpu.VMEM(weight.shape, BF16),
            panel,
            pltpu.VMEM((rows, out_width), F32),
            dma((9,)),
            dma((4,)),
            dma((chunks,)),
            dma((chunks,)),
            dma((chunks,)),
            dma((3,)),
            dma((parts,)),
            dma,
        ]
        + [pltpu.SemaphoreType.REGULAR] * 3,
        compiler_params=pltpu.CompilerParams(collective_id=0, has_side_effects=True, vmem_limit_bytes=48 << 20),
    )(*(pltpu.with_memory_space_constraint(a, pltpu.HBM) for a in (features, tiles, tile_cols, send_rows, recv_dst, recv_weight, recv_count, weight, bias.reshape(1, -1))))


def shifted(array, axis, by):
    size = lax.axis_size(axis)
    return lax.ppermute(array, axis, [(i, (i + by) % size) for i in range(size)])


def ring_layer(features, tiles, tile_cols, send_rows, recv_dst, recv_weight, recv_count, weight, bias):
    cycle_size = lax.axis_size("blk")
    position = lax.axis_index("blk")
    row_blocks = tiles.shape[0]
    tile_rows = tiles.shape[2]
    feature_width = features.shape[1]
    panel_rows = features.shape[0]

    def product(current, source):
        picked = lax.dynamic_index_in_dim(tile_cols, source, 1, keepdims=False)
        matrices = lax.dynamic_index_in_dim(tiles, source, 1, keepdims=False)
        pieces = []
        for row_block in range(row_blocks):
            start = picked[row_block] * tile_rows
            chosen = lax.dynamic_slice_in_dim(current, start, tile_rows, 0)
            pieces.append(jnp.dot(matrices[row_block], chosen, preferred_element_type=jnp.float32))
        return jnp.concatenate(pieces, axis=0)

    summed = product(features, position)

    def advance(rotation, state_carry):
        current, running = state_carry
        current = shifted(current, "blk", 1)
        return (current, running + product(current, (position - rotation) % cycle_size))

    _, summed = lax.fori_loop(1, cycle_size, advance, (features, summed))
    outgoing = features[send_rows[0]]
    incoming = lax.all_to_all(outgoing, "dom", split_axis=0, concat_axis=0, tiled=True)
    slot_ids = jnp.arange(incoming.shape[1])
    in_use = slot_ids[None, :] < recv_count[0][:, None]
    edge_weight = (
        jnp.where(in_use, recv_weight[0], jnp.float32(0.0)).astype(jnp.bfloat16).reshape(1, -1)
    )
    targets = recv_dst[0].reshape(1, -1)
    local_rows = jnp.arange(panel_rows)[:, None]
    placement_matrix = jnp.where(targets == local_rows, edge_weight, jnp.zeros_like(edge_weight))
    summed = summed + jnp.dot(
        placement_matrix, incoming.reshape(-1, feature_width), preferred_element_type=jnp.float32
    )
    aggregated = summed.astype(jnp.bfloat16)
    result = jnp.dot(aggregated, weight, preferred_element_type=jnp.float32) + bias
    return jax.nn.relu(result).astype(jnp.bfloat16)


def solution(mesh):
    in_specs = (
        P(("dom", "blk"), None),
        P(("dom", "blk"), None, None, None),
        P(("dom", "blk"), None),
        P(("dom", "blk"), None, None),
        P(("dom", "blk"), None, None),
        P(("dom", "blk"), None, None),
        P(("dom", "blk"), None),
        P(),
        P(),
    )
    out_specs = P(("dom", "blk"), None)
    layer = line_layer if mesh.shape["blk"] == 4 else ring_layer
    return jax.shard_map(layer, mesh=mesh, in_specs=in_specs, out_specs=out_specs, check_vma=False)
```

```python
import functools

import jax
import jax.numpy as jnp
from jax import lax
from jax.experimental import pallas as pl
from jax.experimental.pallas import tpu as pltpu
from jax.sharding import PartitionSpec as P

CHUNK = 128
LANES = 64
F32 = jnp.float32
BF16 = jnp.bfloat16


def dot(a, b):
    return jnp.dot(a, b, preferred_element_type=F32)


def line_kernel(
    parts,
    feat,
    tiles,
    cols_hbm,
    send_hbm,
    dst_hbm,
    edge_hbm,
    count_hbm,
    weight,
    bias_hbm,
    out,
    cols,
    send_rows,
    recv_dst,
    recv_weight,
    recv_count,
    bias,
    x_own,
    x_par,
    x_om,
    x_oe,
    t_own,
    t_par,
    c_own,
    c_par,
    a_own,
    a_par,
    acc,
    acc_p,
    acc_r,
    packed,
    p_out,
    p_in,
    outgoing,
    incoming,
    place,
    w_vmem,
    agg,
    total,
    load_sem,
    sent,
    first,
    second,
    third,
    tile_recv,
    row_send,
    row_recv,
    end_in,
    mids_in,
    rows_in,
):
    me = lax.axis_index("dom")
    b = lax.axis_index("blk")
    is_end = (b == 0) | (b == 3)
    is_mid = jnp.logical_not(is_end)
    partner = b + 1 - 2 * lax.rem(b, 2)
    across = 3 - b
    far = 3 - partner
    rows, width = x_own.shape
    side = t_own.shape[2]
    blocks = t_own.shape[0]
    slots = outgoing.shape[1]
    chunks = width // CHUNK
    half = rows // 2

    def col(c):
        return pl.ds(pl.multiple_of(c * CHUNK, CHUNK), CHUNK)

    def remote(src, dst, send, recv, target):
        return pltpu.make_async_remote_copy(
            src_ref=src,
            dst_ref=dst,
            send_sem=send,
            recv_sem=recv,
            device_id=target,
            device_id_type=pl.DeviceIdType.MESH,
        )

    def panel_copy(src, dst, send, recv, at, target):
        return remote(src.at[at], dst.at[at], sent.at[send], recv, {"blk": target})

    def chunk(c):
        return (slice(None), col(c))

    last_chunk = chunks - 1
    tail = slice(last_chunk * CHUNK, chunks * CHUNK)

    def piece_rows(j):
        return pl.ds(j * half, half)

    def piece(j):
        return (piece_rows(j), tail)

    def swap(v):
        return pltpu.roll(v, LANES, 1)

    def lower(shape):
        return lax.broadcasted_iota(jnp.int32, shape, 1) < LANES

    def piece_products(a, at, source, j):
        values = source[j * half : (j + 1) * half, tail]
        return dot(a[:, at : at + half], values), dot(a[:, at + half : at + rows], values)

    def x_copy(c):
        return panel_copy(feat, x_par, 0, first.at[c], chunk(c), partner)

    def x_piece(j):
        return remote(packed.at[piece_rows(j)], x_par.at[piece(j)], sent.at[0], first.at[last_chunk + j], {"blk": partner})

    def tile_copy(j):
        source = (far, across)[j]
        return remote(tiles.at[:, source], t_par.at[j], sent.at[1 + j], tile_recv.at[j], {"blk": partner})

    def cols_copy():
        return remote(c_own, c_par, sent.at[3], tile_recv.at[2], {"blk": partner})

    def om_copy(c):
        return panel_copy(feat, x_om, 0, second.at[c], chunk(c), across)

    def om_piece(j):
        return remote(packed.at[piece_rows(j)], x_om.at[piece(j)], sent.at[0], second.at[last_chunk + j], {"blk": across})

    def relay_copy(c):
        return panel_copy(x_par, x_oe, 1, third.at[c], chunk(c), across)

    def relay_piece(j):
        return panel_copy(x_par, x_oe, 1, third.at[last_chunk + j], piece(j), across)

    def y_copy(c):
        return panel_copy(feat, x_par, 2, third.at[c], chunk(c), partner)

    def p_copy(c, h):
        recv = (first, second)[h].at[c]
        return panel_copy(p_out, p_in, 3, recv, (pl.ds(h * half, half), col(c)), partner)

    def all_sent(j, buffer):
        return pltpu.make_async_copy(buffer, buffer, sent.at[j])

    def row_copy(q, k, source):
        return remote(outgoing.at[q], incoming.at[pl.ds(pl.multiple_of(source * slots, slots), slots)], row_send.at[k], row_recv, {"dom": q})

    def load(j, src, dst):
        return pltpu.make_async_copy(src, dst, load_sem.at[j])

    load_cols = load(0, cols_hbm, cols)
    load_x = load(1, feat, x_own)
    load_t = load(2, tiles, t_own)
    load_small = [
        load(3, send_hbm, send_rows),
        load(4, dst_hbm, recv_dst),
        load(5, edge_hbm, recv_weight),
        load(6, count_hbm, recv_count),
        load(7, bias_hbm, bias),
    ]
    load_w = load(8, weight, w_vmem)

    def signal(semaphore, target):
        pl.semaphore_signal(semaphore, inc=1, device_id=target, device_id_type=pl.DeviceIdType.MESH)

    def others(act):
        @pl.loop(1, parts)
        def _(k):
            act({"dom": lax.rem(me + k, parts)})

    barrier = pltpu.get_barrier_semaphore()

    @pl.when(is_mid)
    def _():
        signal(barrier, {"blk": across})
        signal(barrier, {"blk": partner})
        pl.semaphore_wait(barrier, 1)

        @pl.loop(0, last_chunk)
        def _(c):
            om_copy(c).start()

    @pl.when(is_end)
    def _():
        others(lambda target: signal(barrier, target))

    for copy in [load_cols, load_x] + load_small + [load_t, load_w]:
        copy.start()

    @pl.when(is_mid)
    def _():
        pl.semaphore_wait(end_in, 1)

        @pl.loop(0, chunks)
        def _(c):
            y_copy(c).start()

    load_cols.wait()
    for r in range(blocks):
        for s in range(4):
            c_own[pl.ds(r * 4 + s, 1), :] = jnp.full((1, side), cols[r, s], jnp.int32)

    @pl.when(is_end)
    def _():
        pl.semaphore_wait(barrier, parts)
        signal(end_in, {"blk": partner})
        cols_copy().start()
        for j in range(2):
            tile_copy(j).start()

        @pl.loop(0, last_chunk)
        def _(c):
            x_copy(c).start()

        others(lambda target: signal(mids_in, target))

    load_x.wait()
    upper, under = x_own[:half, tail].astype(F32), x_own[half:, tail].astype(F32)
    packed[:half] = jnp.where(lower(upper.shape), upper, swap(under)).astype(BF16)
    packed[half:] = jnp.where(lower(upper.shape), swap(upper), under).astype(BF16)

    @pl.when(is_end)
    def _():
        for j in range(2):
            x_piece(j).start()

    for copy in load_small:
        copy.wait()


    @pl.when(is_end)
    def _():
        pl.semaphore_wait(mids_in, parts - 1)
        signal(rows_in, {"blk": partner})

    @pl.when(is_mid)
    def _():
        pl.semaphore_wait(rows_in, 1)

    row_ids = lax.broadcasted_iota(jnp.int32, (rows, slots), 0)
    slot_ids = lax.broadcasted_iota(jnp.int32, (1, slots), 1)

    @pl.loop(1, parts + 1)
    def _(k):
        q = lax.rem(me + k, parts)
        listed = send_rows[0, pl.ds(q, 1), :]
        hot = jnp.where(row_ids == listed, F32(1.0), F32(0.0)).astype(BF16)
        picked = lax.dot_general(hot, x_own[...], (((0,), (0,)), ((), ())), preferred_element_type=F32)

        @pl.when(k < parts)
        def _():
            outgoing[q] = picked.astype(BF16)


            row_copy(q, k, me).start()

        @pl.when(k == parts)
        def _():
            incoming[pl.ds(pl.multiple_of(me * slots, slots), slots), :] = picked.astype(BF16)

    for q in range(parts):
        used = jnp.where(slot_ids < recv_count[0, q], recv_weight[0, q : q + 1, :], F32(0.0))
        hit = row_ids == recv_dst[0, q : q + 1, :]
        place[:, q * slots : (q + 1) * slots] = jnp.where(hit, used, F32(0.0)).astype(BF16)

    load_t.wait()

    def spread(target, at, matrix, picked, r):
        zero = jnp.zeros_like(matrix)
        mask = jnp.broadcast_to(picked, matrix.shape)
        for block in range(blocks):
            start = at * rows + block * side
            target[r * side : (r + 1) * side, start : start + side] = jnp.where(mask == block, matrix, zero)

    def own_tiles(at, source):
        for r in range(blocks):
            spread(a_own, at, t_own[r, source], c_own[pl.ds(r * 4 + source, 1), :], r)

    def wait_rows():
        arrived = incoming.at[pl.ds(0, (parts - 1) * slots)]
        pltpu.make_async_copy(arrived, arrived, row_recv).wait()

    own_tiles(1, b)
    load_w.wait()
    pair = 2 * CHUNK
    pairs = width // pair

    def pair_at(p):
        return pl.ds(pl.multiple_of(p * pair, pair), pair)

    def add_product(p):
        at = pair_at(p)
        term = dot(agg[:, at], w_vmem[at, :])

        @pl.when(p == 0)
        def _():
            total[...] = term

        @pl.when(p > 0)
        def _():
            total[...] += term

    @pl.when(is_mid)
    def _():
        own_tiles(0, partner)
        own_tiles(2, across)
        own_tiles(3, far)
        cols_copy().wait_recv()
        for j in range(2):
            tile_copy(j).wait_recv()
            source = (across, far)[j]
            for r in range(blocks):
                spread(a_par, j, t_par[j, r], c_par[pl.ds(r * 4 + source, 1), :], r)

        @pl.loop(0, last_chunk + 2)
        def _(step):
            @pl.when(step == last_chunk)
            def _():
                for j in range(2):
                    x_piece(j).wait_recv()
                    om_piece(j).start()
                    relay_piece(j).start()

            @pl.when(step < last_chunk)
            def _():
                at = col(step)
                x_copy(step).wait_recv()
                relay_copy(step).start()
                om_copy(step).wait_recv()
                own = x_own[:, at]
                other = x_om[:, at]
                acc_p[:, at] = dot(a_par[:, :rows], other)
                acc[:, at] = (
                    dot(a_own[:, :rows], x_par[:, at])
                    + dot(a_own[:, rows : 2 * rows], own)
                    + dot(a_own[:, 2 * rows : 3 * rows], other)
                )

            @pl.when(step >= 2)
            def _():
                c = step - 2
                at = col(c)
                relay_copy(c).wait_recv()
                last = x_oe[:, at]
                for h in range(2):
                    part = slice(h * half, (h + 1) * half)
                    p_out[part, at] = (acc_p[part, at] + dot(a_par[part, rows:], last)).astype(BF16)
                    p_copy(c, h).start()
                acc[:, at] += dot(a_own[:, 3 * rows :], last)

            @pl.when(step == 4)
            def _():
                wait_rows()

            @pl.when((step == 4) | (step == 5) | (step == 7))
            def _():
                p = jnp.minimum(step - 4, 2)
                at = pair_at(p)
                agg[:, at] = (acc[:, at] + dot(place[...], incoming[:, at])).astype(BF16)
                add_product(p)

            @pl.when(step == 6)
            def _():
                at = pair_at(pairs - 1)
                acc_r[...] = dot(place[...], incoming[:, at])

        for j in range(2):
            om_piece(j).wait_recv()
            low, high = piece_products(a_par, 0, x_om, j)
            relay_piece(j).wait_recv()
            more_low, more_high = piece_products(a_par, rows, x_oe, j)
            low, high = low + more_low, high + more_high
            p_out[j * half : (j + 1) * half, tail] = jnp.where(
                lower((half, CHUNK)), low[:half] + swap(high[:half]), swap(low[half:]) + high[half:]
            ).astype(BF16)
            p_copy(last_chunk, j).start()

        mine = dot(a_own[:, rows : 2 * rows], x_own[:, tail])
        for j in range(2):
            low, high = piece_products(a_own, 0, x_par, j)
            for at, source in ((2 * rows, x_om), (3 * rows, x_oe)):
                more_low, more_high = piece_products(a_own, at, source, j)
                low, high = low + more_low, high + more_high
            if j == 0:
                both = low + swap(high)
            else:
                mine += jnp.where(lower((rows, CHUNK)), both, swap(low) + high)
        acc[:, tail] = mine
        at = pair_at(pairs - 1)
        agg[:, at] = (acc[:, at] + acc_r[...]).astype(BF16)

    @pl.when(is_end)
    def _():
        own_tiles(0, partner)

        @pl.loop(0, pairs)
        def _(p):
            at = pair_at(p)
            y_copy(2 * p).wait_recv()
            y_copy(2 * p + 1).wait_recv()
            acc[:, at] = dot(a_own[:, rows : 2 * rows], x_own[:, at]) + dot(a_own[:, :rows], x_par[:, at])

        wait_rows()

        @pl.loop(0, pairs)
        def _(p):
            at = pair_at(p)
            acc[:, at] += dot(place[...], incoming[:, at])

        @pl.loop(0, chunks - 1)
        def _(c):
            at = col(c)
            for h in range(2):
                p_copy(c, h).wait_recv()
            agg[:, at] = (acc[:, at] + p_in[:, at].astype(F32)).astype(BF16)

            @pl.when(lax.rem(c, 2) == 1)
            def _():
                add_product(c // 2)

    @pl.when(is_end)
    def _():
        for j in range(2):
            p_copy(last_chunk, j).wait_recv()
        low, high = p_in[:half, tail].astype(F32), p_in[half:, tail].astype(F32)
        agg[:half, tail] = (acc[:half, tail] + jnp.where(lower(low.shape), low, swap(high))).astype(BF16)
        agg[half:, tail] = (acc[half:, tail] + jnp.where(lower(low.shape), swap(low), high)).astype(BF16)

    last = slice((pairs - 1) * pair, pairs * pair)
    for h in range(2):
        part = slice(h * half, (h + 1) * half)
        result = total[part, :] + dot(agg[part, last], w_vmem[last, :]) + bias[...]
        out[part, :] = jnp.maximum(result, F32(0.0)).astype(BF16)

    for k in range(1, parts):
        row_copy(lax.rem(me + k, parts), k, me).wait_send()

    all_sent(0, x_own).wait()

    @pl.when(is_mid)
    def _():
        for j in range(1, 4):
            all_sent(j, x_own).wait()

    @pl.when(is_end)
    def _():
        cols_copy().wait_send()
        for j in range(2):
            tile_copy(j).wait_send()


def line_layer(features, tiles, tile_cols, send_rows, recv_dst, recv_weight, recv_count, weight, bias):
    parts = lax.axis_size("dom")
    rows, width = features.shape
    blocks, group, side, _ = tiles.shape
    slots = send_rows.shape[2]
    chunks = width // CHUNK
    out_width = weight.shape[1]
    hbm = pl.BlockSpec(memory_space=pltpu.HBM)
    dma = pltpu.SemaphoreType.DMA
    panel = pltpu.VMEM((rows, width), BF16)
    return pl.pallas_call(
        functools.partial(line_kernel, parts),
        out_shape=jax.ShapeDtypeStruct((rows, out_width), BF16),
        in_specs=[hbm] * 9,
        out_specs=pl.BlockSpec(memory_space=pltpu.VMEM),
        scratch_shapes=[
            pltpu.SMEM(tile_cols.shape, jnp.int32),
            pltpu.VMEM(send_rows.shape, jnp.int32),
            pltpu.VMEM(recv_dst.shape, jnp.int32),
            pltpu.VMEM(recv_weight.shape, F32),
            pltpu.SMEM(recv_count.shape, jnp.int32),
            pltpu.VMEM((1, out_width), F32),
            panel,
            panel,
            panel,
            panel,
            pltpu.VMEM(tiles.shape, BF16),
            pltpu.VMEM((2, blocks, side, side), BF16),
            pltpu.VMEM((blocks * group, side), jnp.int32),
            pltpu.VMEM((blocks * group, side), jnp.int32),
            pltpu.VMEM((rows, 4 * rows), BF16),
            pltpu.VMEM((rows, 2 * rows), BF16),
            pltpu.VMEM((rows, width), F32),
            pltpu.VMEM((rows, width), F32),
            pltpu.VMEM((rows, 2 * CHUNK), F32),
            pltpu.VMEM((rows, CHUNK), BF16),
            panel,
            panel,
            pltpu.VMEM((parts, slots, width), BF16),
            pltpu.VMEM((parts * slots, width), BF16),
            pltpu.VMEM((rows, parts * slots), BF16),
            pltpu.VMEM(weight.shape, BF16),
            panel,
            pltpu.VMEM((rows, out_width), F32),
            dma((9,)),
            dma((4,)),
            dma((chunks + 1,)),
            dma((chunks + 1,)),
            dma((chunks + 1,)),
            dma((3,)),
            dma((parts,)),
            dma,
        ]
        + [pltpu.SemaphoreType.REGULAR] * 3,
        compiler_params=pltpu.CompilerParams(collective_id=0, has_side_effects=True, vmem_limit_bytes=48 << 20),
    )(*(pltpu.with_memory_space_constraint(a, pltpu.HBM) for a in (features, tiles, tile_cols, send_rows, recv_dst, recv_weight, recv_count, weight, bias.reshape(1, -1))))


def shifted(array, axis, by):
    size = lax.axis_size(axis)
    return lax.ppermute(array, axis, [(i, (i + by) % size) for i in range(size)])


def ring_layer(features, tiles, tile_cols, send_rows, recv_dst, recv_weight, recv_count, weight, bias):
    cycle_size = lax.axis_size("blk")
    position = lax.axis_index("blk")
    row_blocks = tiles.shape[0]
    tile_rows = tiles.shape[2]
    feature_width = features.shape[1]
    panel_rows = features.shape[0]

    def product(current, source):
        picked = lax.dynamic_index_in_dim(tile_cols, source, 1, keepdims=False)
        matrices = lax.dynamic_index_in_dim(tiles, source, 1, keepdims=False)
        pieces = []
        for row_block in range(row_blocks):
            start = picked[row_block] * tile_rows
            chosen = lax.dynamic_slice_in_dim(current, start, tile_rows, 0)
            pieces.append(jnp.dot(matrices[row_block], chosen, preferred_element_type=jnp.float32))
        return jnp.concatenate(pieces, axis=0)

    summed = product(features, position)

    def advance(rotation, state_carry):
        current, running = state_carry
        current = shifted(current, "blk", 1)
        return (current, running + product(current, (position - rotation) % cycle_size))

    _, summed = lax.fori_loop(1, cycle_size, advance, (features, summed))
    outgoing = features[send_rows[0]]
    incoming = lax.all_to_all(outgoing, "dom", split_axis=0, concat_axis=0, tiled=True)
    slot_ids = jnp.arange(incoming.shape[1])
    in_use = slot_ids[None, :] < recv_count[0][:, None]
    edge_weight = (
        jnp.where(in_use, recv_weight[0], jnp.float32(0.0)).astype(jnp.bfloat16).reshape(1, -1)
    )
    targets = recv_dst[0].reshape(1, -1)
    local_rows = jnp.arange(panel_rows)[:, None]
    placement_matrix = jnp.where(targets == local_rows, edge_weight, jnp.zeros_like(edge_weight))
    summed = summed + jnp.dot(
        placement_matrix, incoming.reshape(-1, feature_width), preferred_element_type=jnp.float32
    )
    aggregated = summed.astype(jnp.bfloat16)
    result = jnp.dot(aggregated, weight, preferred_element_type=jnp.float32) + bias
    return jax.nn.relu(result).astype(jnp.bfloat16)


def solution(mesh):
    in_specs = (
        P(("dom", "blk"), None),
        P(("dom", "blk"), None, None, None),
        P(("dom", "blk"), None),
        P(("dom", "blk"), None, None),
        P(("dom", "blk"), None, None),
        P(("dom", "blk"), None, None),
        P(("dom", "blk"), None),
        P(),
        P(),
    )
    out_specs = P(("dom", "blk"), None)
    layer = line_layer if mesh.shape["blk"] == 4 else ring_layer
    return jax.shard_map(layer, mesh=mesh, in_specs=in_specs, out_specs=out_specs, check_vma=False)
```

```python
import functools

import jax
import jax.numpy as jnp
from jax import lax
from jax.experimental import pallas as pl
from jax.experimental.pallas import tpu as pltpu
from jax.sharding import PartitionSpec as P

CHUNK = 128
LANES = 64
F32 = jnp.float32
BF16 = jnp.bfloat16


def dot(a, b):
    return jnp.dot(a, b, preferred_element_type=F32)


def line_kernel(
    parts,
    feat,
    tiles,
    cols_hbm,
    send_hbm,
    dst_hbm,
    edge_hbm,
    count_hbm,
    weight,
    bias_hbm,
    out,
    cols,
    send_rows,
    recv_dst,
    recv_weight,
    recv_count,
    bias,
    x_own,
    x_par,
    x_om,
    x_oe,
    t_own,
    t_par,
    c_own,
    c_par,
    a_own,
    a_par,
    acc,
    acc_p,
    acc_r,
    packed,
    stacked,
    p_out,
    p_in,
    outgoing,
    incoming,
    place,
    w_vmem,
    agg,
    total,
    load_sem,
    sent,
    first,
    second,
    third,
    tile_recv,
    row_send,
    row_recv,
    end_in,
    mids_in,
    rows_in,
):
    me = lax.axis_index("dom")
    b = lax.axis_index("blk")
    is_end = (b == 0) | (b == 3)
    is_mid = jnp.logical_not(is_end)
    partner = b + 1 - 2 * lax.rem(b, 2)
    across = 3 - b
    far = 3 - partner
    rows, width = x_own.shape
    side = t_own.shape[2]
    blocks = t_own.shape[0]
    slots = outgoing.shape[1]
    chunks = width // CHUNK
    half = rows // 2

    def col(c):
        return pl.ds(pl.multiple_of(c * CHUNK, CHUNK), CHUNK)

    def remote(src, dst, send, recv, target):
        return pltpu.make_async_remote_copy(
            src_ref=src,
            dst_ref=dst,
            send_sem=send,
            recv_sem=recv,
            device_id=target,
            device_id_type=pl.DeviceIdType.MESH,
        )

    def panel_copy(src, dst, send, recv, at, target):
        return remote(src.at[at], dst.at[at], sent.at[send], recv, {"blk": target})

    def chunk(c):
        return (slice(None), col(c))

    last_chunk = chunks - 1
    tail = slice(last_chunk * CHUNK, chunks * CHUNK)

    def piece_rows(j):
        return pl.ds(j * half, half)

    def piece(j):
        return (piece_rows(j), tail)

    def swap(v):
        return pltpu.roll(v, LANES, 1)

    def lower(shape):
        return lax.broadcasted_iota(jnp.int32, shape, 1) < LANES

    def packed_sums(at, source, j):
        values = source[j * half : (j + 1) * half, tail]
        stacked[:half] = values
        stacked[half:rows] = swap(values.astype(F32)).astype(BF16)
        stacked[rows:] = values
        top = dot(a_par[:half, at : at + rows], stacked[:rows])
        bottom = dot(a_par[half:, at : at + rows], stacked[half:])
        return jnp.where(lower((half, CHUNK)), top, bottom)

    def piece_products(a, at, source, j):
        values = source[j * half : (j + 1) * half, tail]
        return dot(a[:, at : at + half], values), dot(a[:, at + half : at + rows], values)

    def x_copy(c):
        return panel_copy(feat, x_par, 0, first.at[c], chunk(c), partner)

    def x_piece(j):
        return remote(packed.at[piece_rows(j)], x_par.at[piece(j)], sent.at[0], first.at[last_chunk + j], {"blk": partner})

    def tile_copy(j):
        source = (far, across)[j]
        return remote(tiles.at[:, source], t_par.at[j], sent.at[1 + j], tile_recv.at[j], {"blk": partner})

    def cols_copy():
        return remote(c_own, c_par, sent.at[3], tile_recv.at[2], {"blk": partner})

    def om_copy(c):
        return panel_copy(feat, x_om, 0, second.at[c], chunk(c), across)

    def om_piece(j):
        return remote(packed.at[piece_rows(j)], x_om.at[piece(j)], sent.at[0], second.at[last_chunk + j], {"blk": across})

    def relay_copy(c):
        return panel_copy(x_par, x_oe, 1, third.at[c], chunk(c), across)

    def relay_piece(j):
        return panel_copy(x_par, x_oe, 1, third.at[last_chunk + j], piece(j), across)

    def y_copy(c):
        return panel_copy(feat, x_par, 2, third.at[c], chunk(c), partner)

    def p_copy(c):
        return panel_copy(p_out, p_in, 3, first.at[c], chunk(c), partner)

    def p_piece(j):
        return panel_copy(p_out, p_in, 3, first.at[last_chunk + j], piece(j), partner)

    def all_sent(j, buffer):
        return pltpu.make_async_copy(buffer, buffer, sent.at[j])

    def row_copy(q, source):
        return remote(outgoing.at[q], incoming.at[pl.ds(pl.multiple_of(source * slots, slots), slots)], row_send, row_recv, {"dom": q})

    def load(j, src, dst):
        return pltpu.make_async_copy(src, dst, load_sem.at[j])

    load_cols = load(0, cols_hbm, cols)
    load_x = load(1, feat, x_own)
    load_t = load(2, tiles, t_own)
    load_small = [
        load(3, send_hbm, send_rows),
        load(4, dst_hbm, recv_dst),
        load(5, edge_hbm, recv_weight),
        load(6, count_hbm, recv_count),
        load(7, bias_hbm, bias),
    ]
    load_w = load(8, weight, w_vmem)

    def signal(semaphore, target):
        pl.semaphore_signal(semaphore, inc=1, device_id=target, device_id_type=pl.DeviceIdType.MESH)

    def others(act):
        @pl.loop(1, parts)
        def _(k):
            act({"dom": lax.rem(me + k, parts)})

    barrier = pltpu.get_barrier_semaphore()

    @pl.when(is_mid)
    def _():
        signal(barrier, {"blk": across})
        pl.semaphore_wait(barrier, 1)

        @pl.loop(0, last_chunk)
        def _(c):
            om_copy(c).start()

        signal(barrier, {"blk": partner})

    @pl.when(is_end)
    def _():
        others(lambda target: signal(barrier, target))

    for copy in [load_cols, load_x] + load_small + [load_t, load_w]:
        copy.start()

    @pl.when(is_mid)
    def _():
        pl.semaphore_wait(end_in, 1)

        @pl.loop(0, chunks)
        def _(c):
            y_copy(c).start()

    load_cols.wait()
    for r in range(blocks):
        for s in range(4):
            c_own[pl.ds(r * 4 + s, 1), :] = jnp.full((1, side), cols[r, s], jnp.int32)

    @pl.when(is_end)
    def _():
        pl.semaphore_wait(barrier, parts)
        signal(end_in, {"blk": partner})
        cols_copy().start()
        for j in range(2):
            tile_copy(j).start()

        @pl.loop(0, last_chunk)
        def _(c):
            x_copy(c).start()

        others(lambda target: signal(mids_in, target))

    load_x.wait()
    upper, under = x_own[:half, tail].astype(F32), x_own[half:, tail].astype(F32)
    packed[:half] = jnp.where(lower(upper.shape), upper, swap(under)).astype(BF16)
    packed[half:] = jnp.where(lower(upper.shape), swap(upper), under).astype(BF16)

    @pl.when(is_end)
    def _():
        for j in range(2):
            x_piece(j).start()

    for copy in load_small:
        copy.wait()


    @pl.when(is_end)
    def _():
        pl.semaphore_wait(mids_in, parts - 1)
        signal(rows_in, {"blk": partner})

    @pl.when(is_mid)
    def _():
        pl.semaphore_wait(rows_in, 1)

    row_ids = lax.broadcasted_iota(jnp.int32, (rows, slots), 0)
    slot_ids = lax.broadcasted_iota(jnp.int32, (1, slots), 1)

    @pl.loop(1, parts + 1)
    def _(k):
        q = lax.rem(me + k, parts)
        listed = send_rows[0, pl.ds(q, 1), :]
        hot = jnp.where(row_ids == listed, F32(1.0), F32(0.0)).astype(BF16)
        picked = lax.dot_general(hot, x_own[...], (((0,), (0,)), ((), ())), preferred_element_type=F32)

        @pl.when(k < parts)
        def _():
            outgoing[q] = picked.astype(BF16)


            row_copy(q, me).start()

        @pl.when(k == parts)
        def _():
            incoming[pl.ds(pl.multiple_of(me * slots, slots), slots), :] = picked.astype(BF16)

    for q in range(parts):
        used = jnp.where(slot_ids < recv_count[0, q], recv_weight[0, q : q + 1, :], F32(0.0))
        hit = row_ids == recv_dst[0, q : q + 1, :]
        place[:, q * slots : (q + 1) * slots] = jnp.where(hit, used, F32(0.0)).astype(BF16)

    load_t.wait()

    def spread(target, at, matrix, picked, r):
        zero = jnp.zeros_like(matrix)
        mask = jnp.broadcast_to(picked, matrix.shape)
        for block in range(blocks):
            start = at * rows + block * side
            target[r * side : (r + 1) * side, start : start + side] = jnp.where(mask == block, matrix, zero)

    def own_tiles(at, source):
        for r in range(blocks):
            spread(a_own, at, t_own[r, source], c_own[pl.ds(r * 4 + source, 1), :], r)

    def wait_rows():
        arrived = incoming.at[pl.ds(0, (parts - 1) * slots)]
        pltpu.make_async_copy(arrived, arrived, row_recv).wait()

    own_tiles(1, b)
    load_w.wait()
    pair = 2 * CHUNK
    pairs = width // pair

    def pair_at(p):
        return pl.ds(pl.multiple_of(p * pair, pair), pair)

    def add_product(p):
        at = pair_at(p)
        term = dot(agg[:, at], w_vmem[at, :])

        @pl.when(p == 0)
        def _():
            total[...] = term + bias[...]

        @pl.when(p > 0)
        def _():
            total[...] += term

    @pl.when(is_mid)
    def _():
        own_tiles(0, partner)
        own_tiles(2, across)
        own_tiles(3, far)
        cols_copy().wait_recv()
        for j in range(2):
            tile_copy(j).wait_recv()
            source = (across, far)[j]
            for r in range(blocks):
                spread(a_par, j, t_par[j, r], c_par[pl.ds(r * 4 + source, 1), :], r)

        @pl.loop(0, last_chunk + 2)
        def _(step):
            @pl.when(step == last_chunk)
            def _():
                for j in range(2):
                    x_piece(j).wait_recv()
                    om_piece(j).start()
                    relay_piece(j).start()

            @pl.when(step < last_chunk)
            def _():
                at = col(step)
                x_copy(step).wait_recv()
                relay_copy(step).start()
                om_copy(step).wait_recv()
                own = x_own[:, at]
                other = x_om[:, at]
                acc_p[:, at] = dot(a_par[:, :rows], other)
                acc[:, at] = (
                    dot(a_own[:, :rows], x_par[:, at])
                    + dot(a_own[:, rows : 2 * rows], own)
                    + dot(a_own[:, 2 * rows : 3 * rows], other)
                )

            @pl.when(step >= 2)
            def _():
                c = step - 2
                at = col(c)
                relay_copy(c).wait_recv()
                last = x_oe[:, at]
                p_out[:, at] = (acc_p[:, at] + dot(a_par[:, rows:], last)).astype(BF16)
                p_copy(c).start()
                acc[:, at] += dot(a_own[:, 3 * rows :], last)

            @pl.when(step == 4)
            def _():
                wait_rows()

            @pl.when((step == 4) | (step == 5) | (step == 7))
            def _():
                p = jnp.minimum(step - 4, 2)
                at = pair_at(p)
                agg[:, at] = (acc[:, at] + dot(place[...], incoming[:, at])).astype(BF16)
                add_product(p)

            @pl.when(step == 6)
            def _():
                at = pair_at(pairs - 1)
                acc_r[...] = dot(place[...], incoming[:, at])

        for j in range(2):
            om_piece(j).wait_recv()
            acc_p[:half, tail] = packed_sums(0, x_om, j)
            relay_piece(j).wait_recv()
            p_out[j * half : (j + 1) * half, tail] = (acc_p[:half, tail] + packed_sums(rows, x_oe, j)).astype(BF16)
            p_piece(j).start()

        mine = dot(a_own[:, rows : 2 * rows], x_own[:, tail])
        for j in range(2):
            low, high = piece_products(a_own, 0, x_par, j)
            for at, source in ((2 * rows, x_om), (3 * rows, x_oe)):
                more_low, more_high = piece_products(a_own, at, source, j)
                low, high = low + more_low, high + more_high
            if j == 0:
                both = low + swap(high)
            else:
                mine += jnp.where(lower((rows, CHUNK)), both, swap(low) + high)
        acc[:, tail] = mine
        at = pair_at(pairs - 1)
        agg[:, at] = (acc[:, at] + acc_r[...]).astype(BF16)

    @pl.when(is_end)
    def _():
        own_tiles(0, partner)

        @pl.loop(0, pairs)
        def _(p):
            at = pair_at(p)
            y_copy(2 * p).wait_recv()
            y_copy(2 * p + 1).wait_recv()
            acc[:, at] = dot(a_own[:, rows : 2 * rows], x_own[:, at]) + dot(a_own[:, :rows], x_par[:, at])

        wait_rows()

        @pl.loop(0, pairs)
        def _(p):
            at = pair_at(p)
            acc[:, at] += dot(place[...], incoming[:, at])

        @pl.loop(0, chunks - 1)
        def _(c):
            at = col(c)
            p_copy(c).wait_recv()
            agg[:, at] = (acc[:, at] + p_in[:, at].astype(F32)).astype(BF16)

            @pl.when(lax.rem(c, 2) == 1)
            def _():
                add_product(c // 2)

    @pl.when(is_end)
    def _():
        for j in range(2):
            p_piece(j).wait_recv()
        low, high = p_in[:half, tail].astype(F32), p_in[half:, tail].astype(F32)
        agg[:half, tail] = (acc[:half, tail] + jnp.where(lower(low.shape), low, swap(high))).astype(BF16)
        agg[half:, tail] = (acc[half:, tail] + jnp.where(lower(low.shape), swap(low), high)).astype(BF16)

    last = slice((pairs - 1) * pair, pairs * pair)
    for h in range(2):
        part = slice(h * half, (h + 1) * half)
        result = total[part, :] + dot(agg[part, last], w_vmem[last, :])
        out[part, :] = jnp.maximum(result, F32(0.0)).astype(BF16)

    rows_sent = outgoing.at[pl.ds(0, parts - 1)]
    pltpu.make_async_copy(rows_sent, rows_sent, row_send).wait()

    all_sent(0, x_own).wait()

    @pl.when(is_mid)
    def _():
        for j in range(1, 4):
            all_sent(j, x_own).wait()

    @pl.when(is_end)
    def _():
        cols_copy().wait_send()
        for j in range(2):
            tile_copy(j).wait_send()


def line_layer(features, tiles, tile_cols, send_rows, recv_dst, recv_weight, recv_count, weight, bias):
    parts = lax.axis_size("dom")
    rows, width = features.shape
    blocks, group, side, _ = tiles.shape
    slots = send_rows.shape[2]
    chunks = width // CHUNK
    out_width = weight.shape[1]
    hbm = pl.BlockSpec(memory_space=pltpu.HBM)
    dma = pltpu.SemaphoreType.DMA
    panel = pltpu.VMEM((rows, width), BF16)
    return pl.pallas_call(
        functools.partial(line_kernel, parts),
        out_shape=jax.ShapeDtypeStruct((rows, out_width), BF16),
        in_specs=[hbm] * 9,
        out_specs=pl.BlockSpec(memory_space=pltpu.VMEM),
        scratch_shapes=[
            pltpu.SMEM(tile_cols.shape, jnp.int32),
            pltpu.VMEM(send_rows.shape, jnp.int32),
            pltpu.VMEM(recv_dst.shape, jnp.int32),
            pltpu.VMEM(recv_weight.shape, F32),
            pltpu.SMEM(recv_count.shape, jnp.int32),
            pltpu.VMEM((1, out_width), F32),
            panel,
            panel,
            panel,
            panel,
            pltpu.VMEM(tiles.shape, BF16),
            pltpu.VMEM((2, blocks, side, side), BF16),
            pltpu.VMEM((blocks * group, side), jnp.int32),
            pltpu.VMEM((blocks * group, side), jnp.int32),
            pltpu.VMEM((rows, 4 * rows), BF16),
            pltpu.VMEM((rows, 2 * rows), BF16),
            pltpu.VMEM((rows, width), F32),
            pltpu.VMEM((rows, width), F32),
            pltpu.VMEM((rows, 2 * CHUNK), F32),
            pltpu.VMEM((rows, CHUNK), BF16),
            pltpu.VMEM((rows // 2 * 3, CHUNK), BF16),
            panel,
            panel,
            pltpu.VMEM((parts, slots, width), BF16),
            pltpu.VMEM((parts * slots, width), BF16),
            pltpu.VMEM((rows, parts * slots), BF16),
            pltpu.VMEM(weight.shape, BF16),
            panel,
            pltpu.VMEM((rows, out_width), F32),
            dma((9,)),
            dma((4,)),
            dma((chunks + 1,)),
            dma((chunks + 1,)),
            dma((chunks + 1,)),
            dma((3,)),
            dma,
            dma,
        ]
        + [pltpu.SemaphoreType.REGULAR] * 3,
        compiler_params=pltpu.CompilerParams(collective_id=0, has_side_effects=True, vmem_limit_bytes=48 << 20),
    )(*(pltpu.with_memory_space_constraint(a, pltpu.HBM) for a in (features, tiles, tile_cols, send_rows, recv_dst, recv_weight, recv_count, weight, bias.reshape(1, -1))))


def shifted(array, axis, by):
    size = lax.axis_size(axis)
    return lax.ppermute(array, axis, [(i, (i + by) % size) for i in range(size)])


def ring_layer(features, tiles, tile_cols, send_rows, recv_dst, recv_weight, recv_count, weight, bias):
    cycle_size = lax.axis_size("blk")
    position = lax.axis_index("blk")
    row_blocks = tiles.shape[0]
    tile_rows = tiles.shape[2]
    feature_width = features.shape[1]
    panel_rows = features.shape[0]

    def product(current, source):
        picked = lax.dynamic_index_in_dim(tile_cols, source, 1, keepdims=False)
        matrices = lax.dynamic_index_in_dim(tiles, source, 1, keepdims=False)
        pieces = []
        for row_block in range(row_blocks):
            start = picked[row_block] * tile_rows
            chosen = lax.dynamic_slice_in_dim(current, start, tile_rows, 0)
            pieces.append(jnp.dot(matrices[row_block], chosen, preferred_element_type=jnp.float32))
        return jnp.concatenate(pieces, axis=0)

    summed = product(features, position)

    def advance(rotation, state_carry):
        current, running = state_carry
        current = shifted(current, "blk", 1)
        return (current, running + product(current, (position - rotation) % cycle_size))

    _, summed = lax.fori_loop(1, cycle_size, advance, (features, summed))
    outgoing = features[send_rows[0]]
    incoming = lax.all_to_all(outgoing, "dom", split_axis=0, concat_axis=0, tiled=True)
    slot_ids = jnp.arange(incoming.shape[1])
    in_use = slot_ids[None, :] < recv_count[0][:, None]
    edge_weight = (
        jnp.where(in_use, recv_weight[0], jnp.float32(0.0)).astype(jnp.bfloat16).reshape(1, -1)
    )
    targets = recv_dst[0].reshape(1, -1)
    local_rows = jnp.arange(panel_rows)[:, None]
    placement_matrix = jnp.where(targets == local_rows, edge_weight, jnp.zeros_like(edge_weight))
    summed = summed + jnp.dot(
        placement_matrix, incoming.reshape(-1, feature_width), preferred_element_type=jnp.float32
    )
    aggregated = summed.astype(jnp.bfloat16)
    result = jnp.dot(aggregated, weight, preferred_element_type=jnp.float32) + bias
    return jax.nn.relu(result).astype(jnp.bfloat16)


def solution(mesh):
    in_specs = (
        P(("dom", "blk"), None),
        P(("dom", "blk"), None, None, None),
        P(("dom", "blk"), None),
        P(("dom", "blk"), None, None),
        P(("dom", "blk"), None, None),
        P(("dom", "blk"), None, None),
        P(("dom", "blk"), None),
        P(),
        P(),
    )
    out_specs = P(("dom", "blk"), None)
    layer = line_layer if mesh.shape["blk"] == 4 else ring_layer
    return jax.shard_map(layer, mesh=mesh, in_specs=in_specs, out_specs=out_specs, check_vma=False)
```

```python
import functools

import jax
import jax.numpy as jnp
from jax import lax
from jax.experimental import pallas as pl
from jax.experimental.pallas import tpu as pltpu
from jax.sharding import PartitionSpec as P

CHUNK = 128
LANES = 64
OWN = (0, 2, 4)
F32 = jnp.float32
BF16 = jnp.bfloat16


def dot(a, b):
    return jnp.dot(a, b, preferred_element_type=F32)


def line_kernel(
    parts,
    feat,
    tiles,
    cols_hbm,
    send_hbm,
    dst_hbm,
    edge_hbm,
    count_hbm,
    weight,
    bias_hbm,
    out,
    cols,
    send_rows,
    recv_dst,
    recv_weight,
    recv_count,
    bias,
    x_own,
    x_par,
    x_om,
    x_oe,
    t_own,
    t_par,
    c_own,
    c_par,
    a_own,
    a_par,
    acc,
    acc_p,
    acc_r,
    packed,
    stacked,
    p_out,
    p_in,
    outgoing,
    incoming,
    place,
    w_vmem,
    agg,
    total,
    load_sem,
    sent,
    first,
    second,
    third,
    tile_recv,
    row_send,
    row_recv,
    end_in,
    mids_in,
    rows_in,
):
    me = lax.axis_index("dom")
    b = lax.axis_index("blk")
    is_end = (b == 0) | (b == 3)
    is_mid = jnp.logical_not(is_end)
    partner = b + 1 - 2 * lax.rem(b, 2)
    across = 3 - b
    far = 3 - partner
    rows, width = x_own.shape
    side = t_own.shape[2]
    blocks = t_own.shape[0]
    slots = outgoing.shape[1]
    chunks = width // CHUNK
    half = rows // 2

    pair = 2 * CHUNK
    pairs = width // pair

    def pair_at(p):
        return pl.ds(pl.multiple_of(p * pair, pair), pair)

    def col(c):
        return pl.ds(pl.multiple_of(c * CHUNK, CHUNK), CHUNK)

    def remote(src, dst, send, recv, target):
        return pltpu.make_async_remote_copy(
            src_ref=src,
            dst_ref=dst,
            send_sem=send,
            recv_sem=recv,
            device_id=target,
            device_id_type=pl.DeviceIdType.MESH,
        )

    def panel_copy(src, dst, send, recv, at, target):
        return remote(src.at[at], dst.at[at], sent.at[send], recv, {"blk": target})

    def chunk(c):
        return (slice(None), col(c))

    last_chunk = chunks - 1
    tail = slice(last_chunk * CHUNK, chunks * CHUNK)

    def piece_rows(j):
        return pl.ds(j * half, half)

    def piece(j):
        return (piece_rows(j), tail)

    def swap(v):
        return pltpu.roll(v, LANES, 1)

    def lower(shape):
        return lax.broadcasted_iota(jnp.int32, shape, 1) < LANES

    def packed_sums(at, source, j):
        values = source[j * half : (j + 1) * half, tail]
        stacked[:half] = values
        stacked[half:rows] = swap(values.astype(F32)).astype(BF16)
        stacked[rows:] = values
        top = dot(a_par[:half, at : at + rows], stacked[:rows])
        bottom = dot(a_par[half:, at : at + rows], stacked[half:])
        return jnp.where(lower((half, CHUNK)), top, bottom)

    def piece_products(a, at, source, j):
        values = source[j * half : (j + 1) * half, tail]
        return dot(a[:, at : at + half], values), dot(a[:, at + half : at + rows], values)

    def x_copy(c):
        return panel_copy(feat, x_par, 0, first.at[c], chunk(c), partner)

    def x_piece(j):
        return remote(packed.at[piece_rows(j)], x_par.at[piece(j)], sent.at[0], first.at[last_chunk + j], {"blk": partner})

    def tile_copy(j):
        source = (far, across)[j]
        return remote(tiles.at[:, source], t_par.at[j], sent.at[1 + j], tile_recv.at[j], {"blk": partner})

    def cols_copy():
        return remote(c_own, c_par, sent.at[3], tile_recv.at[2], {"blk": partner})

    def om_copy(c):
        begin, end = (OWN + (last_chunk,))[c : c + 2]
        return panel_copy(feat, x_om, 0, second.at[c], (slice(None), pl.ds(begin * CHUNK, (end - begin) * CHUNK)), across)

    def om_piece(j):
        return remote(packed.at[piece_rows(j)], x_om.at[piece(j)], sent.at[0], second.at[len(OWN) + j], {"blk": across})

    def relay_copy(c):
        return panel_copy(x_par, x_oe, 1, third.at[c], chunk(c), across)

    def relay_piece(j):
        return panel_copy(x_par, x_oe, 1, third.at[last_chunk + j], piece(j), across)

    def y_copy(c):
        return panel_copy(feat, x_par, 2, third.at[c], (slice(None), pair_at(c)), partner)

    def p_copy(c):
        return panel_copy(p_out, p_in, 3, first.at[c], chunk(c), partner)

    def p_piece(j):
        return panel_copy(p_out, p_in, 3, first.at[last_chunk + j], piece(j), partner)

    def all_sent(j, buffer):
        return pltpu.make_async_copy(buffer, buffer, sent.at[j])

    def row_copy(q, source):
        return remote(outgoing.at[q], incoming.at[pl.ds(pl.multiple_of(source * slots, slots), slots)], row_send, row_recv, {"dom": q})

    def load(j, src, dst):
        return pltpu.make_async_copy(src, dst, load_sem.at[j])

    load_cols = load(0, cols_hbm, cols)
    load_x = load(1, feat, x_own)
    load_t = load(2, tiles, t_own)
    load_small = [
        load(3, send_hbm, send_rows),
        load(4, dst_hbm, recv_dst),
        load(5, edge_hbm, recv_weight),
        load(6, count_hbm, recv_count),
        load(7, bias_hbm, bias),
    ]
    load_w = load(8, weight, w_vmem)

    def signal(semaphore, target):
        pl.semaphore_signal(semaphore, inc=1, device_id=target, device_id_type=pl.DeviceIdType.MESH)

    def others(act):
        @pl.loop(1, parts)
        def _(k):
            act({"dom": lax.rem(me + k, parts)})

    barrier = pltpu.get_barrier_semaphore()

    @pl.when(is_mid)
    def _():
        signal(barrier, {"blk": across})
        pl.semaphore_wait(barrier, 1)

        for c in range(len(OWN)):
            om_copy(c).start()

        signal(barrier, {"blk": partner})

    @pl.when(is_end)
    def _():
        others(lambda target: signal(barrier, target))

    for copy in [load_cols, load_x] + load_small + [load_t, load_w]:
        copy.start()

    @pl.when(is_mid)
    def _():
        pl.semaphore_wait(end_in, 1)

        @pl.loop(0, pairs)
        def _(c):
            y_copy(c).start()

    load_cols.wait()
    for r in range(blocks):
        for s in range(4):
            c_own[pl.ds(r * 4 + s, 1), :] = jnp.full((1, side), cols[r, s], jnp.int32)

    @pl.when(is_end)
    def _():
        pl.semaphore_wait(barrier, parts)
        signal(end_in, {"blk": partner})
        cols_copy().start()
        for j in range(2):
            tile_copy(j).start()

        @pl.loop(0, last_chunk)
        def _(c):
            x_copy(c).start()

        others(lambda target: signal(mids_in, target))

    load_x.wait()
    upper, under = x_own[:half, tail].astype(F32), x_own[half:, tail].astype(F32)
    packed[:half] = jnp.where(lower(upper.shape), upper, swap(under)).astype(BF16)
    packed[half:] = jnp.where(lower(upper.shape), swap(upper), under).astype(BF16)

    @pl.when(is_end)
    def _():
        for j in range(2):
            x_piece(j).start()

    for copy in load_small:
        copy.wait()


    @pl.when(is_end)
    def _():
        pl.semaphore_wait(mids_in, parts - 1)
        signal(rows_in, {"blk": partner})

    @pl.when(is_mid)
    def _():
        pl.semaphore_wait(rows_in, 1)

    row_ids = lax.broadcasted_iota(jnp.int32, (rows, slots), 0)
    slot_ids = lax.broadcasted_iota(jnp.int32, (1, slots), 1)

    @pl.loop(1, parts + 1)
    def _(k):
        q = lax.rem(me + k, parts)
        listed = send_rows[0, pl.ds(q, 1), :]
        hot = jnp.where(row_ids == listed, F32(1.0), F32(0.0)).astype(BF16)
        picked = lax.dot_general(hot, x_own[...], (((0,), (0,)), ((), ())), preferred_element_type=F32)

        @pl.when(k < parts)
        def _():
            outgoing[q] = picked.astype(BF16)


            row_copy(q, me).start()

        @pl.when(k == parts)
        def _():
            incoming[pl.ds(pl.multiple_of(me * slots, slots), slots), :] = picked.astype(BF16)

    for q in range(parts):
        used = jnp.where(slot_ids < recv_count[0, q], recv_weight[0, q : q + 1, :], F32(0.0))
        hit = row_ids == recv_dst[0, q : q + 1, :]
        place[:, q * slots : (q + 1) * slots] = jnp.where(hit, used, F32(0.0)).astype(BF16)

    load_t.wait()

    def spread(target, at, matrix, picked, r):
        zero = jnp.zeros_like(matrix)
        mask = jnp.broadcast_to(picked, matrix.shape)
        for block in range(blocks):
            start = at * rows + block * side
            target[r * side : (r + 1) * side, start : start + side] = jnp.where(mask == block, matrix, zero)

    def own_tiles(at, source):
        for r in range(blocks):
            spread(a_own, at, t_own[r, source], c_own[pl.ds(r * 4 + source, 1), :], r)

    def wait_rows():
        arrived = incoming.at[pl.ds(0, (parts - 1) * slots)]
        pltpu.make_async_copy(arrived, arrived, row_recv).wait()

    own_tiles(1, b)
    load_w.wait()
    def add_product(p):
        at = pair_at(p)
        term = dot(agg[:, at], w_vmem[at, :])

        @pl.when(p == 0)
        def _():
            total[...] = term + bias[...]

        @pl.when(p > 0)
        def _():
            total[...] += term

    @pl.when(is_mid)
    def _():
        own_tiles(0, partner)
        own_tiles(2, across)
        own_tiles(3, far)
        cols_copy().wait_recv()
        for j in range(2):
            tile_copy(j).wait_recv()
            source = (across, far)[j]
            for r in range(blocks):
                spread(a_par, j, t_par[j, r], c_par[pl.ds(r * 4 + source, 1), :], r)

        @pl.loop(0, last_chunk + 2)
        def _(step):
            @pl.when(step == last_chunk)
            def _():
                for j in range(2):
                    x_piece(j).wait_recv()
                    om_piece(j).start()
                    relay_piece(j).start()

            @pl.when(step < last_chunk)
            def _():
                at = col(step)
                x_copy(step).wait_recv()
                relay_copy(step).start()
                for c in range(len(OWN)):

                    @pl.when(step == OWN[c])
                    def _():
                        om_copy(c).wait_recv()

                own = x_own[:, at]
                other = x_om[:, at]
                acc_p[:, at] = dot(a_par[:, :rows], other)
                acc[:, at] = (
                    dot(a_own[:, :rows], x_par[:, at])
                    + dot(a_own[:, rows : 2 * rows], own)
                    + dot(a_own[:, 2 * rows : 3 * rows], other)
                )

            @pl.when(step >= 2)
            def _():
                c = step - 2
                at = col(c)
                relay_copy(c).wait_recv()
                last = x_oe[:, at]
                p_out[:, at] = (acc_p[:, at] + dot(a_par[:, rows:], last)).astype(BF16)
                p_copy(c).start()
                acc[:, at] += dot(a_own[:, 3 * rows :], last)

            @pl.when(step == 4)
            def _():
                wait_rows()

            @pl.when((step == 4) | (step == 5) | (step == 7))
            def _():
                p = jnp.minimum(step - 4, 2)
                at = pair_at(p)
                agg[:, at] = (acc[:, at] + dot(place[...], incoming[:, at])).astype(BF16)
                add_product(p)

            @pl.when(step == 6)
            def _():
                at = pair_at(pairs - 1)
                acc_r[...] = dot(place[...], incoming[:, at])

        for j in range(2):
            om_piece(j).wait_recv()
            acc_p[:half, tail] = packed_sums(0, x_om, j)
            relay_piece(j).wait_recv()
            p_out[j * half : (j + 1) * half, tail] = (acc_p[:half, tail] + packed_sums(rows, x_oe, j)).astype(BF16)
            p_piece(j).start()

        mine = dot(a_own[:, rows : 2 * rows], x_own[:, tail])
        for j in range(2):
            low, high = piece_products(a_own, 0, x_par, j)
            for at, source in ((2 * rows, x_om), (3 * rows, x_oe)):
                more_low, more_high = piece_products(a_own, at, source, j)
                low, high = low + more_low, high + more_high
            if j == 0:
                both = low + swap(high)
            else:
                mine += jnp.where(lower((rows, CHUNK)), both, swap(low) + high)
        acc[:, tail] = mine
        at = pair_at(pairs - 1)
        agg[:, at] = (acc[:, at] + acc_r[...]).astype(BF16)

    @pl.when(is_end)
    def _():
        own_tiles(0, partner)

        @pl.loop(0, pairs)
        def _(p):
            at = pair_at(p)
            y_copy(p).wait_recv()
            acc[:, at] = dot(a_own[:, rows : 2 * rows], x_own[:, at]) + dot(a_own[:, :rows], x_par[:, at])

        wait_rows()

        @pl.loop(0, pairs)
        def _(p):
            at = pair_at(p)
            acc[:, at] += dot(place[...], incoming[:, at])

        @pl.loop(0, chunks - 1)
        def _(c):
            at = col(c)
            p_copy(c).wait_recv()
            agg[:, at] = (acc[:, at] + p_in[:, at].astype(F32)).astype(BF16)

            @pl.when(lax.rem(c, 2) == 1)
            def _():
                add_product(c // 2)

    @pl.when(is_end)
    def _():
        for j in range(2):
            p_piece(j).wait_recv()
        low, high = p_in[:half, tail].astype(F32), p_in[half:, tail].astype(F32)
        agg[:half, tail] = (acc[:half, tail] + jnp.where(lower(low.shape), low, swap(high))).astype(BF16)
        agg[half:, tail] = (acc[half:, tail] + jnp.where(lower(low.shape), swap(low), high)).astype(BF16)

    last = slice((pairs - 1) * pair, pairs * pair)
    for h in range(2):
        part = slice(h * half, (h + 1) * half)
        result = total[part, :] + dot(agg[part, last], w_vmem[last, :])
        out[part, :] = jnp.maximum(result, F32(0.0)).astype(BF16)

    rows_sent = outgoing.at[pl.ds(0, parts - 1)]
    pltpu.make_async_copy(rows_sent, rows_sent, row_send).wait()

    all_sent(0, x_own).wait()

    @pl.when(is_mid)
    def _():
        for j in range(1, 4):
            all_sent(j, x_own).wait()

    @pl.when(is_end)
    def _():
        cols_copy().wait_send()
        for j in range(2):
            tile_copy(j).wait_send()


def line_layer(features, tiles, tile_cols, send_rows, recv_dst, recv_weight, recv_count, weight, bias):
    parts = lax.axis_size("dom")
    rows, width = features.shape
    blocks, group, side, _ = tiles.shape
    slots = send_rows.shape[2]
    chunks = width // CHUNK
    out_width = weight.shape[1]
    hbm = pl.BlockSpec(memory_space=pltpu.HBM)
    dma = pltpu.SemaphoreType.DMA
    panel = pltpu.VMEM((rows, width), BF16)
    return pl.pallas_call(
        functools.partial(line_kernel, parts),
        out_shape=jax.ShapeDtypeStruct((rows, out_width), BF16),
        in_specs=[hbm] * 9,
        out_specs=pl.BlockSpec(memory_space=pltpu.VMEM),
        scratch_shapes=[
            pltpu.SMEM(tile_cols.shape, jnp.int32),
            pltpu.VMEM(send_rows.shape, jnp.int32),
            pltpu.VMEM(recv_dst.shape, jnp.int32),
            pltpu.VMEM(recv_weight.shape, F32),
            pltpu.SMEM(recv_count.shape, jnp.int32),
            pltpu.VMEM((1, out_width), F32),
            panel,
            panel,
            panel,
            panel,
            pltpu.VMEM(tiles.shape, BF16),
            pltpu.VMEM((2, blocks, side, side), BF16),
            pltpu.VMEM((blocks * group, side), jnp.int32),
            pltpu.VMEM((blocks * group, side), jnp.int32),
            pltpu.VMEM((rows, 4 * rows), BF16),
            pltpu.VMEM((rows, 2 * rows), BF16),
            pltpu.VMEM((rows, width), F32),
            pltpu.VMEM((rows, width), F32),
            pltpu.VMEM((rows, 2 * CHUNK), F32),
            pltpu.VMEM((rows, CHUNK), BF16),
            pltpu.VMEM((rows // 2 * 3, CHUNK), BF16),
            panel,
            panel,
            pltpu.VMEM((parts, slots, width), BF16),
            pltpu.VMEM((parts * slots, width), BF16),
            pltpu.VMEM((rows, parts * slots), BF16),
            pltpu.VMEM(weight.shape, BF16),
            panel,
            pltpu.VMEM((rows, out_width), F32),
            dma((9,)),
            dma((4,)),
            dma((chunks + 1,)),
            dma((len(OWN) + 2,)),
            dma((chunks + 1,)),
            dma((3,)),
            dma,
            dma,
        ]
        + [pltpu.SemaphoreType.REGULAR] * 3,
        compiler_params=pltpu.CompilerParams(collective_id=0, has_side_effects=True, vmem_limit_bytes=48 << 20),
    )(*(pltpu.with_memory_space_constraint(a, pltpu.HBM) for a in (features, tiles, tile_cols, send_rows, recv_dst, recv_weight, recv_count, weight, bias.reshape(1, -1))))


def shifted(array, axis, by):
    size = lax.axis_size(axis)
    return lax.ppermute(array, axis, [(i, (i + by) % size) for i in range(size)])


def ring_layer(features, tiles, tile_cols, send_rows, recv_dst, recv_weight, recv_count, weight, bias):
    cycle_size = lax.axis_size("blk")
    position = lax.axis_index("blk")
    row_blocks = tiles.shape[0]
    tile_rows = tiles.shape[2]
    feature_width = features.shape[1]
    panel_rows = features.shape[0]

    def product(current, source):
        picked = lax.dynamic_index_in_dim(tile_cols, source, 1, keepdims=False)
        matrices = lax.dynamic_index_in_dim(tiles, source, 1, keepdims=False)
        pieces = []
        for row_block in range(row_blocks):
            start = picked[row_block] * tile_rows
            chosen = lax.dynamic_slice_in_dim(current, start, tile_rows, 0)
            pieces.append(jnp.dot(matrices[row_block], chosen, preferred_element_type=jnp.float32))
        return jnp.concatenate(pieces, axis=0)

    summed = product(features, position)

    def advance(rotation, state_carry):
        current, running = state_carry
        current = shifted(current, "blk", 1)
        return (current, running + product(current, (position - rotation) % cycle_size))

    _, summed = lax.fori_loop(1, cycle_size, advance, (features, summed))
    outgoing = features[send_rows[0]]
    incoming = lax.all_to_all(outgoing, "dom", split_axis=0, concat_axis=0, tiled=True)
    slot_ids = jnp.arange(incoming.shape[1])
    in_use = slot_ids[None, :] < recv_count[0][:, None]
    edge_weight = (
        jnp.where(in_use, recv_weight[0], jnp.float32(0.0)).astype(jnp.bfloat16).reshape(1, -1)
    )
    targets = recv_dst[0].reshape(1, -1)
    local_rows = jnp.arange(panel_rows)[:, None]
    placement_matrix = jnp.where(targets == local_rows, edge_weight, jnp.zeros_like(edge_weight))
    summed = summed + jnp.dot(
        placement_matrix, incoming.reshape(-1, feature_width), preferred_element_type=jnp.float32
    )
    aggregated = summed.astype(jnp.bfloat16)
    result = jnp.dot(aggregated, weight, preferred_element_type=jnp.float32) + bias
    return jax.nn.relu(result).astype(jnp.bfloat16)


def solution(mesh):
    in_specs = (
        P(("dom", "blk"), None),
        P(("dom", "blk"), None, None, None),
        P(("dom", "blk"), None),
        P(("dom", "blk"), None, None),
        P(("dom", "blk"), None, None),
        P(("dom", "blk"), None, None),
        P(("dom", "blk"), None),
        P(),
        P(),
    )
    out_specs = P(("dom", "blk"), None)
    layer = line_layer if mesh.shape["blk"] == 4 else ring_layer
    return jax.shard_map(layer, mesh=mesh, in_specs=in_specs, out_specs=out_specs, check_vma=False)
```

```python
import functools

import jax
import jax.numpy as jnp
from jax import lax
from jax.experimental import pallas as pl
from jax.experimental.pallas import tpu as pltpu
from jax.sharding import PartitionSpec as P

CHUNK = 128
LANES = 64
F32 = jnp.float32
BF16 = jnp.bfloat16


def dot(a, b):
    return jnp.dot(a, b, preferred_element_type=F32)


def line_kernel(
    parts,
    feat,
    tiles,
    cols_hbm,
    send_hbm,
    dst_hbm,
    edge_hbm,
    count_hbm,
    weight,
    bias_hbm,
    out,
    cols,
    send_rows,
    recv_dst,
    recv_weight,
    recv_count,
    bias,
    x_own,
    x_par,
    x_om,
    x_oe,
    t_own,
    t_par,
    c_own,
    c_par,
    a_own,
    a_par,
    acc,
    acc_p,
    acc_r,
    packed,
    stacked,
    p_out,
    p_in,
    outgoing,
    incoming,
    place,
    w_vmem,
    agg,
    total,
    load_sem,
    sent,
    first,
    second,
    third,
    tile_recv,
    row_send,
    row_recv,
    end_in,
    mids_in,
    rows_in,
):
    me = lax.axis_index("dom")
    b = lax.axis_index("blk")
    is_end = (b == 0) | (b == 3)
    is_mid = jnp.logical_not(is_end)
    partner = b + 1 - 2 * lax.rem(b, 2)
    across = 3 - b
    far = 3 - partner
    rows, width = x_own.shape
    side = t_own.shape[2]
    blocks = t_own.shape[0]
    slots = outgoing.shape[1]
    chunks = width // CHUNK
    half = rows // 2

    def col(c):
        return pl.ds(pl.multiple_of(c * CHUNK, CHUNK), CHUNK)

    def remote(src, dst, send, recv, target):
        return pltpu.make_async_remote_copy(
            src_ref=src,
            dst_ref=dst,
            send_sem=send,
            recv_sem=recv,
            device_id=target,
            device_id_type=pl.DeviceIdType.MESH,
        )

    def panel_copy(src, dst, send, recv, at, target):
        return remote(src.at[at], dst.at[at], sent.at[send], recv, {"blk": target})

    def chunk(c):
        return (slice(None), col(c))

    last_chunk = chunks - 1
    tail = slice(last_chunk * CHUNK, chunks * CHUNK)

    def piece_rows(j):
        return pl.ds(j * half, half)

    def piece(j):
        return (piece_rows(j), tail)

    def swap(v):
        return pltpu.roll(v, LANES, 1)

    def lower(shape):
        return lax.broadcasted_iota(jnp.int32, shape, 1) < LANES

    def packed_sums(at, source, j):
        values = source[j * half : (j + 1) * half, tail]
        stacked[:half] = values
        stacked[half:rows] = swap(values.astype(F32)).astype(BF16)
        stacked[rows:] = values
        top = dot(a_par[:half, at : at + rows], stacked[:rows])
        bottom = dot(a_par[half:, at : at + rows], stacked[half:])
        return jnp.where(lower((half, CHUNK)), top, bottom)

    def piece_products(a, at, source, j):
        values = source[j * half : (j + 1) * half, tail]
        return dot(a[:, at : at + half], values), dot(a[:, at + half : at + rows], values)

    def x_copy(c):
        return panel_copy(feat, x_par, 0, first.at[c], chunk(c), partner)

    def x_piece(j):
        return remote(packed.at[piece_rows(j)], x_par.at[piece(j)], sent.at[0], first.at[last_chunk + j], {"blk": partner})

    def tile_copy(j):
        source = (far, across)[j]
        return remote(tiles.at[:, source], t_par.at[j], sent.at[1 + j], tile_recv.at[j], {"blk": partner})

    def cols_copy():
        return remote(c_own, c_par, sent.at[3], tile_recv.at[2], {"blk": partner})

    def om_copy(c):
        return panel_copy(feat, x_om, 0, second.at[c], chunk(c), across)

    def om_piece(j):
        return remote(packed.at[piece_rows(j)], x_om.at[piece(j)], sent.at[0], second.at[last_chunk + j], {"blk": across})

    def relay_copy(c):
        return panel_copy(x_par, x_oe, 1, third.at[c], chunk(c), across)

    def relay_piece(j):
        return panel_copy(x_par, x_oe, 1, third.at[last_chunk + j], piece(j), across)

    def y_copy(c):
        return panel_copy(feat, x_par, 2, third.at[c], chunk(c), partner)

    def p_copy(c):
        return panel_copy(p_out, p_in, 3, first.at[c], chunk(c), partner)

    def p_piece(j):
        return panel_copy(p_out, p_in, 3, first.at[last_chunk + j], piece(j), partner)

    def all_sent(j, buffer):
        return pltpu.make_async_copy(buffer, buffer, sent.at[j])

    def row_copy(q, source):
        return remote(outgoing.at[q], incoming.at[pl.ds(pl.multiple_of(source * slots, slots), slots)], row_send, row_recv, {"dom": q})

    def load(j, src, dst):
        return pltpu.make_async_copy(src, dst, load_sem.at[j])

    load_cols = load(0, cols_hbm, cols)
    load_x = load(1, feat, x_own)
    load_t = load(2, tiles, t_own)
    load_small = [
        load(3, send_hbm, send_rows),
        load(4, dst_hbm, recv_dst),
        load(5, edge_hbm, recv_weight),
        load(6, count_hbm, recv_count),
        load(7, bias_hbm, bias),
    ]
    load_w = load(8, weight, w_vmem)

    def signal(semaphore, target):
        pl.semaphore_signal(semaphore, inc=1, device_id=target, device_id_type=pl.DeviceIdType.MESH)

    def others(act):
        @pl.loop(1, parts)
        def _(k):
            act({"dom": lax.rem(me + k, parts)})

    barrier = pltpu.get_barrier_semaphore()

    @pl.when(is_mid)
    def _():
        signal(barrier, {"blk": across})
        pl.semaphore_wait(barrier, 1)

        @pl.loop(0, last_chunk)
        def _(c):
            om_copy(c).start()

        signal(barrier, {"blk": partner})

    @pl.when(is_end)
    def _():
        others(lambda target: signal(barrier, target))

    for copy in [load_cols, load_x] + load_small + [load_t]:
        copy.start()

    @pl.when(is_mid)
    def _():
        pl.semaphore_wait(end_in, 1)

        @pl.loop(0, chunks)
        def _(c):
            y_copy(c).start()

    load_cols.wait()
    for r in range(blocks):
        for s in range(4):
            c_own[pl.ds(r * 4 + s, 1), :] = jnp.full((1, side), cols[r, s], jnp.int32)

    @pl.when(is_end)
    def _():
        pl.semaphore_wait(barrier, parts)
        signal(end_in, {"blk": partner})
        cols_copy().start()
        for j in range(2):
            tile_copy(j).start()

        @pl.loop(0, last_chunk)
        def _(c):
            x_copy(c).start()

        others(lambda target: signal(mids_in, target))

    load_x.wait()
    upper, under = x_own[:half, tail].astype(F32), x_own[half:, tail].astype(F32)
    packed[:half] = jnp.where(lower(upper.shape), upper, swap(under)).astype(BF16)
    packed[half:] = jnp.where(lower(upper.shape), swap(upper), under).astype(BF16)

    @pl.when(is_end)
    def _():
        for j in range(2):
            x_piece(j).start()

    for copy in load_small:
        copy.wait()


    @pl.when(is_end)
    def _():
        pl.semaphore_wait(mids_in, parts - 1)
        signal(rows_in, {"blk": partner})

    @pl.when(is_mid)
    def _():
        pl.semaphore_wait(rows_in, 1)

    row_ids = lax.broadcasted_iota(jnp.int32, (rows, slots), 0)
    slot_ids = lax.broadcasted_iota(jnp.int32, (1, slots), 1)

    @pl.loop(1, parts + 1)
    def _(k):
        q = lax.rem(me + k, parts)
        listed = send_rows[0, pl.ds(q, 1), :]
        hot = jnp.where(row_ids == listed, F32(1.0), F32(0.0)).astype(BF16)
        picked = lax.dot_general(hot, x_own[...], (((0,), (0,)), ((), ())), preferred_element_type=F32)

        @pl.when(k < parts)
        def _():
            outgoing[q] = picked.astype(BF16)


            row_copy(q, me).start()

        @pl.when(k == parts)
        def _():
            incoming[pl.ds(pl.multiple_of(me * slots, slots), slots), :] = picked.astype(BF16)

    load_w.start()

    for q in range(parts):
        used = jnp.where(slot_ids < recv_count[0, q], recv_weight[0, q : q + 1, :], F32(0.0))
        hit = row_ids == recv_dst[0, q : q + 1, :]
        place[:, q * slots : (q + 1) * slots] = jnp.where(hit, used, F32(0.0)).astype(BF16)

    load_t.wait()

    def spread(target, at, matrix, picked, r):
        zero = jnp.zeros_like(matrix)
        mask = jnp.broadcast_to(picked, matrix.shape)
        for block in range(blocks):
            start = at * rows + block * side
            target[r * side : (r + 1) * side, start : start + side] = jnp.where(mask == block, matrix, zero)

    def own_tiles(at, source):
        for r in range(blocks):
            spread(a_own, at, t_own[r, source], c_own[pl.ds(r * 4 + source, 1), :], r)

    def wait_rows():
        arrived = incoming.at[pl.ds(0, (parts - 1) * slots)]
        pltpu.make_async_copy(arrived, arrived, row_recv).wait()

    own_tiles(1, b)
    load_w.wait()
    pair = 2 * CHUNK
    pairs = width // pair

    def pair_at(p):
        return pl.ds(pl.multiple_of(p * pair, pair), pair)

    def add_product(p):
        at = pair_at(p)
        term = dot(agg[:, at], w_vmem[at, :])

        @pl.when(p == 0)
        def _():
            total[...] = term + bias[...]

        @pl.when(p > 0)
        def _():
            total[...] += term

    @pl.when(is_mid)
    def _():
        own_tiles(0, partner)
        own_tiles(2, across)
        own_tiles(3, far)
        cols_copy().wait_recv()
        for j in range(2):
            tile_copy(j).wait_recv()
            source = (across, far)[j]
            for r in range(blocks):
                spread(a_par, j, t_par[j, r], c_par[pl.ds(r * 4 + source, 1), :], r)

        @pl.loop(0, last_chunk + 2)
        def _(step):
            @pl.when(step == last_chunk)
            def _():
                for j in range(2):
                    x_piece(j).wait_recv()
                    om_piece(j).start()
                    relay_piece(j).start()

            @pl.when(step < last_chunk)
            def _():
                at = col(step)
                x_copy(step).wait_recv()
                relay_copy(step).start()
                om_copy(step).wait_recv()
                own = x_own[:, at]
                other = x_om[:, at]
                acc_p[:, at] = dot(a_par[:, :rows], other)
                acc[:, at] = (
                    dot(a_own[:, :rows], x_par[:, at])
                    + dot(a_own[:, rows : 2 * rows], own)
                    + dot(a_own[:, 2 * rows : 3 * rows], other)
                )

            @pl.when(step >= 2)
            def _():
                c = step - 2
                at = col(c)
                relay_copy(c).wait_recv()
                last = x_oe[:, at]
                p_out[:, at] = (acc_p[:, at] + dot(a_par[:, rows:], last)).astype(BF16)
                p_copy(c).start()
                acc[:, at] += dot(a_own[:, 3 * rows :], last)

            @pl.when(step == 4)
            def _():
                wait_rows()

            @pl.when((step == 4) | (step == 5) | (step == 7))
            def _():
                p = jnp.minimum(step - 4, 2)
                at = pair_at(p)
                agg[:, at] = (acc[:, at] + dot(place[...], incoming[:, at])).astype(BF16)
                add_product(p)

            @pl.when(step == 6)
            def _():
                at = pair_at(pairs - 1)
                acc_r[...] = dot(place[...], incoming[:, at])

        for j in range(2):
            om_piece(j).wait_recv()
            acc_p[:half, tail] = packed_sums(0, x_om, j)
            relay_piece(j).wait_recv()
            p_out[j * half : (j + 1) * half, tail] = (acc_p[:half, tail] + packed_sums(rows, x_oe, j)).astype(BF16)
            p_piece(j).start()

        mine = dot(a_own[:, rows : 2 * rows], x_own[:, tail])
        for j in range(2):
            low, high = piece_products(a_own, 0, x_par, j)
            for at, source in ((2 * rows, x_om), (3 * rows, x_oe)):
                more_low, more_high = piece_products(a_own, at, source, j)
                low, high = low + more_low, high + more_high
            if j == 0:
                both = low + swap(high)
            else:
                mine += jnp.where(lower((rows, CHUNK)), both, swap(low) + high)
        acc[:, tail] = mine
        at = pair_at(pairs - 1)
        agg[:, at] = (acc[:, at] + acc_r[...]).astype(BF16)

    @pl.when(is_end)
    def _():
        own_tiles(0, partner)

        @pl.loop(0, pairs)
        def _(p):
            at = pair_at(p)
            y_copy(2 * p).wait_recv()
            y_copy(2 * p + 1).wait_recv()
            acc[:, at] = dot(a_own[:, rows : 2 * rows], x_own[:, at]) + dot(a_own[:, :rows], x_par[:, at])

        wait_rows()

        @pl.loop(0, pairs)
        def _(p):
            at = pair_at(p)
            acc[:, at] += dot(place[...], incoming[:, at])

        @pl.loop(0, chunks - 1)
        def _(c):
            at = col(c)
            p_copy(c).wait_recv()
            agg[:, at] = (acc[:, at] + p_in[:, at].astype(F32)).astype(BF16)

            @pl.when(lax.rem(c, 2) == 1)
            def _():
                add_product(c // 2)

    @pl.when(is_end)
    def _():
        for j in range(2):
            p_piece(j).wait_recv()
        low, high = p_in[:half, tail].astype(F32), p_in[half:, tail].astype(F32)
        agg[:half, tail] = (acc[:half, tail] + jnp.where(lower(low.shape), low, swap(high))).astype(BF16)
        agg[half:, tail] = (acc[half:, tail] + jnp.where(lower(low.shape), swap(low), high)).astype(BF16)

    last = slice((pairs - 1) * pair, pairs * pair)
    for h in range(2):
        part = slice(h * half, (h + 1) * half)
        result = total[part, :] + dot(agg[part, last], w_vmem[last, :])
        out[part, :] = jnp.maximum(result, F32(0.0)).astype(BF16)

    rows_sent = outgoing.at[pl.ds(0, parts - 1)]
    pltpu.make_async_copy(rows_sent, rows_sent, row_send).wait()

    all_sent(0, x_own).wait()

    @pl.when(is_mid)
    def _():
        for j in range(1, 4):
            all_sent(j, x_own).wait()

    @pl.when(is_end)
    def _():
        cols_copy().wait_send()
        for j in range(2):
            tile_copy(j).wait_send()


def line_layer(features, tiles, tile_cols, send_rows, recv_dst, recv_weight, recv_count, weight, bias):
    parts = lax.axis_size("dom")
    rows, width = features.shape
    blocks, group, side, _ = tiles.shape
    slots = send_rows.shape[2]
    chunks = width // CHUNK
    out_width = weight.shape[1]
    hbm = pl.BlockSpec(memory_space=pltpu.HBM)
    dma = pltpu.SemaphoreType.DMA
    panel = pltpu.VMEM((rows, width), BF16)
    return pl.pallas_call(
        functools.partial(line_kernel, parts),
        out_shape=jax.ShapeDtypeStruct((rows, out_width), BF16),
        in_specs=[hbm] * 9,
        out_specs=pl.BlockSpec(memory_space=pltpu.VMEM),
        scratch_shapes=[
            pltpu.SMEM(tile_cols.shape, jnp.int32),
            pltpu.VMEM(send_rows.shape, jnp.int32),
            pltpu.VMEM(recv_dst.shape, jnp.int32),
            pltpu.VMEM(recv_weight.shape, F32),
            pltpu.SMEM(recv_count.shape, jnp.int32),
            pltpu.VMEM((1, out_width), F32),
            panel,
            panel,
            panel,
            panel,
            pltpu.VMEM(tiles.shape, BF16),
            pltpu.VMEM((2, blocks, side, side), BF16),
            pltpu.VMEM((blocks * group, side), jnp.int32),
            pltpu.VMEM((blocks * group, side), jnp.int32),
            pltpu.VMEM((rows, 4 * rows), BF16),
            pltpu.VMEM((rows, 2 * rows), BF16),
            pltpu.VMEM((rows, width), F32),
            pltpu.VMEM((rows, width), F32),
            pltpu.VMEM((rows, 2 * CHUNK), F32),
            pltpu.VMEM((rows, CHUNK), BF16),
            pltpu.VMEM((rows // 2 * 3, CHUNK), BF16),
            panel,
            panel,
            pltpu.VMEM((parts, slots, width), BF16),
            pltpu.VMEM((parts * slots, width), BF16),
            pltpu.VMEM((rows, parts * slots), BF16),
            pltpu.VMEM(weight.shape, BF16),
            panel,
            pltpu.VMEM((rows, out_width), F32),
            dma((9,)),
            dma((4,)),
            dma((chunks + 1,)),
            dma((chunks + 1,)),
            dma((chunks + 1,)),
            dma((3,)),
            dma,
            dma,
        ]
        + [pltpu.SemaphoreType.REGULAR] * 3,
        compiler_params=pltpu.CompilerParams(collective_id=0, has_side_effects=True, vmem_limit_bytes=48 << 20),
    )(*(pltpu.with_memory_space_constraint(a, pltpu.HBM) for a in (features, tiles, tile_cols, send_rows, recv_dst, recv_weight, recv_count, weight, bias.reshape(1, -1))))


def shifted(array, axis, by):
    size = lax.axis_size(axis)
    return lax.ppermute(array, axis, [(i, (i + by) % size) for i in range(size)])


def ring_layer(features, tiles, tile_cols, send_rows, recv_dst, recv_weight, recv_count, weight, bias):
    cycle_size = lax.axis_size("blk")
    position = lax.axis_index("blk")
    row_blocks = tiles.shape[0]
    tile_rows = tiles.shape[2]
    feature_width = features.shape[1]
    panel_rows = features.shape[0]

    def product(current, source):
        picked = lax.dynamic_index_in_dim(tile_cols, source, 1, keepdims=False)
        matrices = lax.dynamic_index_in_dim(tiles, source, 1, keepdims=False)
        pieces = []
        for row_block in range(row_blocks):
            start = picked[row_block] * tile_rows
            chosen = lax.dynamic_slice_in_dim(current, start, tile_rows, 0)
            pieces.append(jnp.dot(matrices[row_block], chosen, preferred_element_type=jnp.float32))
        return jnp.concatenate(pieces, axis=0)

    summed = product(features, position)

    def advance(rotation, state_carry):
        current, running = state_carry
        current = shifted(current, "blk", 1)
        return (current, running + product(current, (position - rotation) % cycle_size))

    _, summed = lax.fori_loop(1, cycle_size, advance, (features, summed))
    outgoing = features[send_rows[0]]
    incoming = lax.all_to_all(outgoing, "dom", split_axis=0, concat_axis=0, tiled=True)
    slot_ids = jnp.arange(incoming.shape[1])
    in_use = slot_ids[None, :] < recv_count[0][:, None]
    edge_weight = (
        jnp.where(in_use, recv_weight[0], jnp.float32(0.0)).astype(jnp.bfloat16).reshape(1, -1)
    )
    targets = recv_dst[0].reshape(1, -1)
    local_rows = jnp.arange(panel_rows)[:, None]
    placement_matrix = jnp.where(targets == local_rows, edge_weight, jnp.zeros_like(edge_weight))
    summed = summed + jnp.dot(
        placement_matrix, incoming.reshape(-1, feature_width), preferred_element_type=jnp.float32
    )
    aggregated = summed.astype(jnp.bfloat16)
    result = jnp.dot(aggregated, weight, preferred_element_type=jnp.float32) + bias
    return jax.nn.relu(result).astype(jnp.bfloat16)


def solution(mesh):
    in_specs = (
        P(("dom", "blk"), None),
        P(("dom", "blk"), None, None, None),
        P(("dom", "blk"), None),
        P(("dom", "blk"), None, None),
        P(("dom", "blk"), None, None),
        P(("dom", "blk"), None, None),
        P(("dom", "blk"), None),
        P(),
        P(),
    )
    out_specs = P(("dom", "blk"), None)
    layer = line_layer if mesh.shape["blk"] == 4 else ring_layer
    return jax.shard_map(layer, mesh=mesh, in_specs=in_specs, out_specs=out_specs, check_vma=False)
```
